32 devices in a mesh: site: 8 (over z, y), rhs: 4 (over x, core).
Axes of the slice: x: 2, y: 2, z: 4, core: 2. Of those that a mesh axis runs over, the one named last changes fastest.
Arguments:
- rhs_vecs: bfloat16 [128, 128, 128], P(None, ('site', 'rhs')), may hold values from -8 to 8, as said below
- deflation: bfloat16 [256, 128, 128], P(None, ('site', 'rhs')), may hold values from -6 to 6
- coarse_inverse: float32 [2, 256, 256], replicated, may hold values from -4.5776367e-05 to 4.5776367e-05
- coupling: bfloat16 [128, 9, 128, 128], P('site'), may hold values from -1 to 5, as said below
- neighbours: int32 [128, 8], P('site'), may hold values from 0 to 127, as said below
- grouping: int32 [128], replicated, may hold values from 0 to 127, each once
Outputs:
- solution: float32 [128, 128, 128], P('rhs', 'site')
- residual: float32 [128, 128, 128], P('rhs', 'site')
The draws below stay inside these ranges and needn't reach their ends.
Inputs may be any that keep to these rules, and one draw needn't show every extreme that they name: `rhs_vecs`: mean zero, site scales differ from site to site. `coupling`: the self block's real part carries a real diagonal between 2 and 4.2 added to small blocks. Entry m of a site's row lies within 8 positions of the site along the cyclic site order, after it for even m and before it for odd m; in every draw some site has neighbours exactly 8 positions away in both directions.
All inputs are finite; a program needn't handle non-finite values.
Results may differ from the reference program's by a relative error of at most 0.01.
Values may be sent and summed in bfloat16 or wider, within the bound.
A program may use at most 64 MiB of HBM per device.

```python
import math
import jax
import jax.numpy as jnp
from jax import lax

C = 128
K = 256
RHS = 128
MR_STEPS = 2
SITES_DEV = 16
SITES = 128
REACH = 8
N_SITE = 8


def draw_rhs_vecs(key, part):
    first_key, second_key = jax.random.split(jax.random.fold_in(key, 7), 2)
    values = jnp.clip(jax.random.normal(first_key, (RHS, SITES, C), jnp.float32), -4.0, 4.0)
    rough = jnp.exp(jax.random.uniform(second_key, (1, SITES, 1), jnp.float32, -0.7, 0.7))
    rising = 1.0 + 2.0 * jnp.arange(SITES, dtype=jnp.float32)[None, :, None] / SITES
    return jnp.clip(values * rough * rising, -8.0, 8.0).astype(jnp.bfloat16)


def draw_coupling(key, part):
    first_key, second_key = jax.random.split(jax.random.fold_in(key, 11), 2)
    half_width = C // 2
    sigma = 0.4 / math.sqrt(half_width)
    pieces = jnp.clip(jax.random.normal(first_key, (2, SITES, 9, half_width, half_width), jnp.float32), -4.0, 4.0) * sigma
    diagonal = 3.0 * jnp.exp(jax.random.uniform(second_key, (SITES,), jnp.float32, math.log(0.7), math.log(1.4)))
    identity = jnp.eye(half_width, dtype=jnp.float32)
    self_mask = (jnp.arange(9) == 0).astype(jnp.float32)
    real_part = pieces[0] + diagonal[:, None, None, None] * self_mask[None, :, None, None] * identity[None, None, :, :]
    imag_part = pieces[1]
    upper = jnp.concatenate([real_part, imag_part], axis=-1)
    lower = jnp.concatenate([-imag_part, real_part], axis=-1)
    return jnp.concatenate([upper, lower], axis=-2).astype(jnp.bfloat16)


def draw_neighbours(key, part):
    first_key, second_key = jax.random.split(jax.random.fold_in(key, 23), 2)
    distance = jax.random.randint(first_key, (SITES, 8), 1, REACH + 1)
    picked = jax.random.randint(second_key, (), 0, SITES)
    row_index = jnp.arange(SITES, dtype=jnp.int32)[:, None]
    col_index = jnp.arange(8, dtype=jnp.int32)[None, :]
    distance = jnp.where((row_index == picked) & (col_index < 2), REACH, distance)
    direction_sign = jnp.where(col_index % 2 == 0, 1, -1)
    return ((row_index + direction_sign * distance) % SITES).astype(jnp.int32)


def raised(entries, own_key, source, target, parts, factor):
    def block_of(dim):
        return (jnp.arange(entries.shape[dim]) // (entries.shape[dim] // parts)).reshape((-1,) + (1,) * (entries.ndim - 1 - dim))

    first = jax.random.permutation(own_key, parts)[block_of(target)]
    second = (block_of(target) + parts // 2) % parts
    return jnp.where((block_of(source) == first) | (block_of(source) == second), factor * entries, entries)


def block_scale(key, extent, cuts, least, largest):
    gain = 1.0
    for axis_at, shards_of in cuts:
        heights = jax.random.uniform(jax.random.fold_in(jax.random.fold_in(key, 6), axis_at), (shards_of,), jnp.float32, least / len(cuts), largest / len(cuts))
        gain = gain * jnp.repeat(jnp.exp(heights), extent[axis_at] // shards_of).reshape((-1,) + (1,) * (len(extent) - 1 - axis_at))
    return gain


def noise(key, dims, deviation, reach, cuts=(), held_as=jnp.bfloat16):
    array = jax.random.normal(key, dims, jnp.float32) * deviation
    if len(cuts) > 0:
        array = block_scale(key, dims, cuts, -0.22, 0.18) * array
    return jnp.clip(array, min=-reach, max=reach).astype(held_as)


def heavy_noise(own_key, extent, spread, most, cuts, heavy, kind=jnp.bfloat16):
    values = spread * jax.random.normal(own_key, extent, jnp.float32)
    if cuts:
        values = values * block_scale(own_key, extent, cuts, -0.22, 0.18)
    return jnp.clip(raised(values, jax.random.fold_in(own_key, 3), *heavy), -most, most).astype(kind)


def setup_inputs(seed: int = 0) -> dict:
    streams_of = jax.random.split(jax.random.key(seed), 7)
    rhs_vecs = draw_rhs_vecs(jax.random.fold_in(streams_of[6], 71), 0)
    deflation = heavy_noise(streams_of[1], (K, SITES, C), 1.0, 6.0, ((1, 32),), (1, 0, 32, 2.75))
    coarse_inverse = noise(streams_of[2], (2, K, K), (16 * K * K * SITES * C) ** -0.5, 4.57763671875e-05, (), jnp.float32)
    coupling = draw_coupling(jax.random.fold_in(streams_of[6], 71), 0)
    neighbours = draw_neighbours(jax.random.fold_in(streams_of[6], 71), 0)
    grouping = jax.random.permutation(streams_of[5], RHS).astype(jnp.int32)
    return dict(rhs_vecs=rhs_vecs, deflation=deflation, coarse_inverse=coarse_inverse, coupling=coupling, neighbours=neighbours, grouping=grouping)


def turned(vectors):
    half_width = vectors.shape[-1] // 2
    return jnp.concatenate([-vectors[..., half_width:], vectors[..., :half_width]], axis=-1)


def conj_turned(vectors):
    half_width = vectors.shape[-1] // 2
    return jnp.concatenate([vectors[..., half_width:], -vectors[..., :half_width]], axis=-1)


def scaled(alpha_re, alpha_im, vectors):
    return alpha_re[:, None, None] * vectors + alpha_im[:, None, None] * turned(vectors)


def operate(vectors, coupling, neighbours):
    slots = vectors.shape[0]
    width = vectors.shape[2]

    def one_block(block_index):
        first = (block_index * SITES_DEV).astype(jnp.int32)
        table = lax.dynamic_slice_in_dim(neighbours, first, SITES_DEV, 0)
        blocks = lax.dynamic_slice_in_dim(coupling, first, SITES_DEV, 0)
        own = lax.dynamic_slice_in_dim(vectors, first, SITES_DEV, 1)
        beside = jnp.take(vectors, table.reshape(-1), axis=1).reshape(slots, SITES_DEV, 8, width)
        stacked = jnp.concatenate([own[:, :, None, :], beside], axis=2).astype(jnp.float32)
        stacked = stacked.reshape(slots, SITES_DEV, 9 * width)
        matrices = blocks.astype(jnp.float32).reshape(SITES_DEV, 9 * width, width)
        return jnp.einsum("rsi,sio->rso", stacked, matrices)

    result = lax.map(one_block, jnp.arange(N_SITE, dtype=jnp.int32))
    return jnp.transpose(result, (1, 0, 2, 3)).reshape(slots, N_SITE * SITES_DEV, width)


def reference(rhs_vecs, deflation, coarse_inverse, coupling, neighbours, grouping):
    highest = lax.Precision.HIGHEST
    ordered = jnp.take(rhs_vecs, grouping, axis=0)
    basis = deflation.astype(jnp.float32)
    given = ordered.astype(jnp.float32)
    coef_re = jnp.einsum("ksc,rsc->kr", basis, given)
    coef_im = jnp.einsum("ksc,rsc->kr", basis, conj_turned(given))
    real_part = coarse_inverse[0]
    imag_part = coarse_inverse[1]
    solved_re = jnp.dot(real_part, coef_re, precision=highest, preferred_element_type=jnp.float32) - jnp.dot(imag_part, coef_im, precision=highest, preferred_element_type=jnp.float32)
    solved_im = jnp.dot(real_part, coef_im, precision=highest, preferred_element_type=jnp.float32) + jnp.dot(imag_part, coef_re, precision=highest, preferred_element_type=jnp.float32)
    low_re = solved_re.astype(jnp.bfloat16).astype(jnp.float32)
    low_im = solved_im.astype(jnp.bfloat16).astype(jnp.float32)
    start = jnp.einsum("kr,ksc->rsc", low_re, basis) + jnp.einsum("kr,ksc->rsc", low_im, turned(basis))
    start_low = start.astype(jnp.bfloat16)
    solution = start_low.astype(jnp.float32)
    residual = given - operate(start_low, coupling, neighbours)
    for iteration in range(MR_STEPS):
        image = operate(residual.astype(jnp.bfloat16), coupling, neighbours)
        upper_re = jnp.sum(image * residual, axis=(1, 2))
        upper_im = jnp.sum(image * conj_turned(residual), axis=(1, 2))
        lower = jnp.sum(image * image, axis=(1, 2))
        alpha_re = upper_re / lower
        alpha_im = upper_im / lower
        solution = solution + scaled(alpha_re, alpha_im, residual)
        residual = residual - scaled(alpha_re, alpha_im, image)
    return solution, residual
```

```python
import functools

import jax
import jax.numpy as jnp
from jax import lax
from jax.experimental import pallas as pl
from jax.experimental.pallas import tpu as pltpu
from jax.sharding import PartitionSpec as P

MESH = pl.DeviceIdType.MESH
MR_STEPS = 2


def extended_2(array, sides, width):
    for axis, dim in sides:
        size, length = (lax.axis_size(axis), array.shape[dim])
        up = [(i, (i + 1) % size) for i in range(size)]
        down = [(j, i) for i, j in up]
        last = lax.slice_in_dim(array, length - width, length, axis=dim)
        first = lax.slice_in_dim(array, 0, width, axis=dim)
        before = lax.ppermute(last, axis, up)
        after = lax.ppermute(first, axis, down)
        array = jnp.concatenate([before, array, after], axis=dim)
    return array


def turned(vectors):
    half_width = vectors.shape[-1] // 2
    return jnp.concatenate([-vectors[..., half_width:], vectors[..., :half_width]], axis=-1)


def conj_turned(vectors):
    half_width = vectors.shape[-1] // 2
    return jnp.concatenate([vectors[..., half_width:], -vectors[..., :half_width]], axis=-1)


def scaled(alpha_re, alpha_im, vectors):
    return alpha_re[:, None, None] * vectors + alpha_im[:, None, None] * turned(vectors)


def small_solve(coarse_inverse, coef_re, coef_im):
    highest = lax.Precision.HIGHEST
    real_part = coarse_inverse[0]
    imag_part = coarse_inverse[1]
    solved_re = jnp.dot(
        real_part, coef_re, precision=highest, preferred_element_type=jnp.float32
    ) - jnp.dot(imag_part, coef_im, precision=highest, preferred_element_type=jnp.float32)
    solved_im = jnp.dot(
        real_part, coef_im, precision=highest, preferred_element_type=jnp.float32
    ) + jnp.dot(imag_part, coef_re, precision=highest, preferred_element_type=jnp.float32)
    return (solved_re, solved_im)


def operate(vectors, coupling, neighbours):
    slots = vectors.shape[0]
    sites_here = vectors.shape[1]
    width = vectors.shape[2]
    reach = sites_here // 2
    extended = extended_2(vectors, (("site", 1),), reach)
    anchor = lax.axis_index("site") * sites_here
    total = sites_here * lax.axis_size("site")
    position = (neighbours - anchor + reach) % total
    beside = jnp.take(extended, position.reshape(-1), axis=1).reshape(slots, sites_here, 8, width)
    stacked = jnp.concatenate([vectors[:, :, None, :], beside], axis=2).reshape(
        slots, sites_here, 9 * width
    )
    blocks = coupling.reshape(sites_here, 9 * width, width)
    product = lax.dot_general(
        stacked, blocks, (((2,), (1,)), ((1,), (0,))), preferred_element_type=jnp.float32
    )
    return jnp.transpose(product, (1, 0, 2))


def staged(rhs_vecs, deflation, coarse_inverse, coupling, neighbours, grouping):
    ordered = jnp.take(rhs_vecs, grouping, axis=0)
    coef_re = jnp.einsum("ksc,rsc->kr", deflation, ordered, preferred_element_type=jnp.float32)
    coef_im = jnp.einsum(
        "ksc,rsc->kr", deflation, conj_turned(ordered), preferred_element_type=jnp.float32
    )
    group_re, group_im = (
        lax.psum_scatter(coef_re, "rhs", scatter_dimension=1, tiled=True),
        lax.psum_scatter(coef_im, "rhs", scatter_dimension=1, tiled=True),
    )
    group_re, group_im = lax.psum((group_re, group_im), "site")
    share_re, share_im = small_solve(coarse_inverse, group_re, group_im)
    solved_re, solved_im = (
        lax.all_gather(share_re.astype(jnp.bfloat16), "rhs", axis=1, tiled=True).astype(
            share_re.dtype
        ),
        lax.all_gather(share_im.astype(jnp.bfloat16), "rhs", axis=1, tiled=True).astype(
            share_im.dtype
        ),
    )
    low_re = solved_re.astype(jnp.bfloat16)
    low_im = solved_im.astype(jnp.bfloat16)
    start = jnp.einsum("kr,ksc->rsc", low_re, deflation, preferred_element_type=jnp.float32)
    start = start + jnp.einsum(
        "kr,ksc->rsc", low_im, turned(deflation), preferred_element_type=jnp.float32
    )
    start_low = start.astype(jnp.bfloat16)
    given_low, placed = (
        lax.all_to_all(ordered, "rhs", split_axis=0, concat_axis=1, tiled=True),
        lax.all_to_all(start_low, "rhs", split_axis=0, concat_axis=1, tiled=True),
    )
    given = given_low.astype(jnp.float32)
    solution = placed.astype(jnp.float32)
    residual = given - operate(placed, coupling, neighbours)
    for iteration in range(MR_STEPS):
        image = operate(residual.astype(jnp.bfloat16), coupling, neighbours)
        upper_re = jnp.sum(image * residual, axis=(1, 2))
        upper_im = jnp.sum(image * conj_turned(residual), axis=(1, 2))
        lower = jnp.sum(image * image, axis=(1, 2))
        upper_re, upper_im, lower = lax.psum((upper_re, upper_im, lower), "site")
        alpha_re = upper_re / lower
        alpha_im = upper_im / lower
        solution = solution + scaled(alpha_re, alpha_im, residual)
        residual = residual - scaled(alpha_re, alpha_im, image)
    return (solution, residual)


def lanes_turned(values, conj):
    width = values.shape[-1]
    lane = lax.broadcasted_iota(jnp.int32, values.shape, values.ndim - 1)
    rolled = pltpu.roll(values, width // 2, values.ndim - 1)
    low = lane < width // 2
    if conj:
        return jnp.where(low, rolled, -rolled)
    return jnp.where(low, -rolled, rolled)


def fused_kernel(
    n_site, n_rhs,
    rhs_ref, defl_ref, inv_ref, coup_hbm, nb_ref, group_ref,
    sol_ref, res_ref,
    coup, gathered, ordered, given, coef, parts, solved, solved_all, ext0, ext1, ext2, image, sums, sums_all,
    coup_sem, coef_send, coef_recv, pack_send, pack_recv, defl_send, defl_recv,
    solved_send, solved_recv, halo_send, halo_recv, sums_send, sums_recv,
):
    devices = n_site * n_rhs
    sites_local, slots, width = rhs_ref.shape
    sites_here = coup_hbm.shape[0]
    reach = sites_here // 2
    group = slots // n_rhs
    share = group // n_site
    vecs = defl_ref.shape[1]
    f32, bf16 = jnp.float32, jnp.bfloat16
    exts = (ext0, ext1, ext2)

    my_site = lax.axis_index("site")
    my_rhs = lax.axis_index("rhs")
    me = my_rhs * n_site + my_site

    def peer(d):
        at = lax.rem(me + d, devices)
        return at, (lax.rem(at, n_site), at // n_site)

    barrier = pltpu.get_barrier_semaphore()

    def greet(d, carry):
        _, dev = peer(d)
        pl.semaphore_signal(barrier, inc=1, device_id=dev, device_id_type=MESH)
        return carry

    lax.fori_loop(1, devices, greet, 0)
    load_coup = pltpu.make_async_copy(coup_hbm, coup, coup_sem)
    load_coup.start()

    row = lax.broadcasted_iota(jnp.int32, (slots, slots), 0)
    placed = jnp.where(row == group_ref[...], 1.0, 0.0).astype(f32)
    placed = jnp.transpose(placed).astype(bf16)
    row2 = lax.broadcasted_iota(jnp.int32, (2 * slots, slots), 0)
    col2 = lax.broadcasted_iota(jnp.int32, (2 * slots, slots), 1)
    spread = jnp.where(col2 == (row2 // (2 * share)) * share + row2 % share, 1.0, 0.0).astype(bf16)
    part = (lax.broadcasted_iota(jnp.int32, (2 * slots, width), 0) // share) % 2
    both = []
    for i in range(sites_local):
        g = jnp.dot(placed, rhs_ref[i], preferred_element_type=f32).astype(bf16)
        ordered[i] = g
        two = jnp.dot(spread, g, preferred_element_type=f32)
        both.append(jnp.where(part == 1, lanes_turned(two, True), two).astype(bf16))
    both = jnp.concatenate(both, axis=1)
    basis = jnp.concatenate([defl_ref[i] for i in range(sites_local)], axis=1)
    total = lax.dot_general(both, basis, (((1,), (1,)), ((), ())), preferred_element_type=f32)
    coef[...] = total.reshape(devices, 2 * share, vecs)

    pl.semaphore_wait(barrier, devices - 1)

    def coef_copy(d):
        at, dev = peer(d)
        return pltpu.make_async_remote_copy(
            src_ref=coef.at[at], dst_ref=parts.at[me], send_sem=coef_send.at[d],
            recv_sem=coef_recv.at[me], device_id=dev, device_id_type=MESH)

    def coef_start(d, carry):
        coef_copy(d).start()
        return carry

    lax.fori_loop(1, devices, coef_start, 0)

    packs, defls = [], []
    for d in range(1, n_rhs):
        other = lax.rem(my_rhs + d, n_rhs)
        packs.append(pltpu.make_async_remote_copy(
            src_ref=ordered.at[:, pl.ds(pl.multiple_of(other * group, group), group), :],
            dst_ref=given.at[pl.ds(my_rhs * sites_local, sites_local)],
            send_sem=pack_send.at[d], recv_sem=pack_recv.at[d],
            device_id=(my_site, other), device_id_type=MESH))
        defls.append(pltpu.make_async_remote_copy(
            src_ref=defl_ref,
            dst_ref=gathered.at[pl.ds(my_rhs * sites_local, sites_local)],
            send_sem=defl_send.at[d], recv_sem=defl_recv.at[d],
            device_id=(my_site, other), device_id_type=MESH))
    for copy in packs + defls:
        copy.start()
    given[pl.ds(my_rhs * sites_local, sites_local)] = ordered[:, pl.ds(pl.multiple_of(my_rhs * group, group), group), :]
    gathered[pl.ds(my_rhs * sites_local, sites_local)] = defl_ref[...]
    parts[me] = coef[me]

    def coef_wait(d, carry):
        at, dev = peer(d)
        pltpu.make_async_remote_copy(
            src_ref=coef.at[at], dst_ref=parts.at[at], send_sem=coef_send.at[d],
            recv_sem=coef_recv.at[at], device_id=dev, device_id_type=MESH).wait_recv()
        return carry

    lax.fori_loop(1, devices, coef_wait, 0)
    mine = jnp.sum(parts[...], axis=0)
    swapped = pltpu.roll(mine, share, 0)
    first = lax.broadcasted_iota(jnp.int32, mine.shape, 0) < share
    swapped = jnp.where(first, -swapped, swapped)
    nt = (((1,), (1,)), ((), ()))
    out = lax.dot_general(mine, inv_ref[0], nt, precision=lax.Precision.HIGHEST, preferred_element_type=f32)
    out = out + lax.dot_general(swapped, inv_ref[1], nt, precision=lax.Precision.HIGHEST, preferred_element_type=f32)
    solved[...] = out

    def along(d):
        return lax.rem(my_site + d, n_site)

    def to_all_sites(src, dst, send, recv):
        copies = []
        for d in range(1, n_site):
            copies.append(pltpu.make_async_remote_copy(
                src_ref=src, dst_ref=dst.at[my_site], send_sem=send.at[d],
                recv_sem=recv.at[d], device_id=(along(d), my_rhs), device_id_type=MESH))
        for copy in copies:
            copy.start()
        dst[my_site] = src[...]
        return copies

    copies = to_all_sites(solved, solved_all, solved_send, solved_recv)

    def coef_sent(d, carry):
        coef_copy(d).wait_send()
        return carry

    lax.fori_loop(1, devices, coef_sent, 0)
    row3 = lax.broadcasted_iota(jnp.int32, (2 * group, 2 * group), 0)
    col3 = lax.broadcasted_iota(jnp.int32, (2 * group, 2 * group), 1)
    slot3 = row3 % group
    want = (slot3 // share) * (2 * share) + (row3 // group) * share + slot3 % share
    sort = jnp.where(col3 == want, 1.0, 0.0).astype(bf16)
    for copy in copies:
        copy.wait()
    low = solved_all[...].reshape(2 * group, vecs).astype(bf16)
    low = jnp.dot(sort, low, preferred_element_type=f32).astype(bf16)
    for copy in packs + defls:
        copy.wait()
    for i in range(sites_here):
        z = jnp.dot(low, gathered[i], preferred_element_type=f32)
        start = (z[:group] + lanes_turned(z[group:], False)).astype(bf16)
        ext0[reach + i] = start
        sol_ref[i] = start.astype(f32)

    def halo(step):
        buf = exts[step]
        up = pltpu.make_async_remote_copy(
            src_ref=buf.at[pl.ds(sites_here, reach)], dst_ref=buf.at[pl.ds(0, reach)],
            send_sem=halo_send.at[2 * step], recv_sem=halo_recv.at[2 * step],
            device_id=(along(1), my_rhs), device_id_type=MESH)
        down = pltpu.make_async_remote_copy(
            src_ref=buf.at[pl.ds(reach, reach)], dst_ref=buf.at[pl.ds(reach + sites_here, reach)],
            send_sem=halo_send.at[2 * step + 1], recv_sem=halo_recv.at[2 * step + 1],
            device_id=(along(n_site - 1), my_rhs), device_id_type=MESH)
        up.start()
        down.start()
        return up, down

    anchor = my_site * sites_here - reach

    def operate(step, i):
        pieces = [exts[step][reach + i]]
        for m in range(nb_ref.shape[1]):
            at = (nb_ref[i, m] - anchor) & (2 * sites_here - 1)
            pieces.append(exts[step][at])
        stacked = jnp.concatenate(pieces, axis=1)
        return jnp.dot(stacked, coup[i], preferred_element_type=f32)

    copies = halo(0)
    load_coup.wait()
    for copy in copies:
        copy.wait()
    for i in range(sites_here):
        r = given[i].astype(f32) - operate(0, i)
        res_ref[i] = r
        ext1[reach + i] = r.astype(bf16)

    lane = lax.broadcasted_iota(jnp.int32, (8, width), 1)
    bands = group // 8
    for step in range(2):
        for copy in halo(step + 1):
            copy.wait()
        tops = [jnp.zeros((group, width), f32) for _ in range(3)]
        for i in range(sites_here):
            y = operate(step + 1, i)
            r = res_ref[i]
            image[i] = y
            tops[0] = tops[0] + y * r
            tops[1] = tops[1] + y * lanes_turned(r, True)
            tops[2] = tops[2] + y * y
        tile = jnp.zeros((8, width), f32)
        for v in range(3):
            column = jnp.sum(tops[v], axis=1, keepdims=True)
            for b in range(bands):
                tile = jnp.where(lane == 3 * b + v, column[8 * b:8 * b + 8], tile)
        sums[step] = tile
        for copy in to_all_sites(sums.at[step], sums_all.at[step], sums_send.at[step], sums_recv.at[step]):
            copy.wait()
        tile = jnp.sum(sums_all[step], axis=0)
        values = []
        for v in range(3):
            values.append(jnp.concatenate([tile[:, 3 * b + v:3 * b + v + 1] for b in range(bands)], axis=0))
        alpha_re = values[0] / values[2]
        alpha_im = values[1] / values[2]
        for i in range(sites_here):
            r, y = res_ref[i], image[i]
            sol_ref[i] = sol_ref[i] + (alpha_re * r + alpha_im * lanes_turned(r, False))
            r = r - (alpha_re * y + alpha_im * lanes_turned(y, False))
            res_ref[i] = r
            if step == 0:
                ext2[reach + i] = r.astype(bf16)


def fused(n_site, n_rhs, rhs_vecs, deflation, coarse_inverse, coupling, neighbours, grouping):
    f32, bf16 = jnp.float32, jnp.bfloat16
    slots, sites_local, width = rhs_vecs.shape
    vecs = deflation.shape[0]
    sites_here = coupling.shape[0]
    group = slots // n_rhs
    share = group // n_site
    devices = n_site * n_rhs
    blocks = coupling.reshape(sites_here, -1, width)
    vmem = pl.BlockSpec(memory_space=pltpu.VMEM)
    out = jax.ShapeDtypeStruct((sites_here, group, width), f32)
    dma = pltpu.SemaphoreType.DMA
    sol, res = pl.pallas_call(
        functools.partial(fused_kernel, n_site, n_rhs),
        out_shape=(out, out),
        in_specs=[vmem, vmem, vmem, pl.BlockSpec(memory_space=pl.ANY),
                  pl.BlockSpec(memory_space=pltpu.SMEM), vmem],
        out_specs=(vmem, vmem),
        scratch_shapes=[
            pltpu.VMEM(blocks.shape, bf16),
            pltpu.VMEM((sites_here, vecs, width), bf16),
            pltpu.VMEM((sites_local, slots, width), bf16),
            pltpu.VMEM((sites_here, group, width), bf16),
            pltpu.VMEM((devices, 2 * share, vecs), f32),
            pltpu.VMEM((devices, 2 * share, vecs), f32),
            pltpu.VMEM((2 * share, vecs), f32),
            pltpu.VMEM((n_site, 2 * share, vecs), f32),
            pltpu.VMEM((2 * sites_here, group, width), bf16),
            pltpu.VMEM((2 * sites_here, group, width), bf16),
            pltpu.VMEM((2 * sites_here, group, width), bf16),
            pltpu.VMEM((sites_here, group, width), f32),
            pltpu.VMEM((2, 8, width), f32),
            pltpu.VMEM((2, n_site, 8, width), f32),
            dma, dma((devices,)), dma((devices,)), dma((n_rhs,)), dma((n_rhs,)),
            dma((n_rhs,)), dma((n_rhs,)), dma((n_site,)), dma((n_site,)),
            dma((6,)), dma((6,)), dma((2, n_site)), dma((2, n_site)),
        ],
        compiler_params=pltpu.CompilerParams(
            collective_id=0, has_side_effects=True, vmem_limit_bytes=40 * 1024 * 1024),
    )(
        jnp.transpose(rhs_vecs, (1, 0, 2)),
        jnp.transpose(deflation, (1, 0, 2)),
        coarse_inverse,
        blocks,
        neighbours,
        grouping.reshape(1, slots),
    )
    return jnp.transpose(sol, (1, 0, 2)), jnp.transpose(res, (1, 0, 2))


def fits(n_site, n_rhs, rhs_vecs, coupling):
    slots, sites_local, width = rhs_vecs.shape
    sites_here = coupling.shape[0]
    group = slots // n_rhs
    share = group // n_site
    return (
        share * n_site * n_rhs == slots
        and (2 * share) % 8 == 0
        and group % 16 == 0
        and 3 * (group // 8) <= width
        and slots % 128 == 0
        and width % 128 == 0
        and sites_local * n_rhs == sites_here
        and n_site >= 3
        and n_site % 2 == 0
        and sites_here & (sites_here - 1) == 0
    )


def per_device(n_site, n_rhs, *arrays):
    if fits(n_site, n_rhs, arrays[0], arrays[3]):
        return fused(n_site, n_rhs, *arrays)
    return staged(*arrays)


def solution(mesh):
    return jax.shard_map(
        functools.partial(per_device, mesh.shape["site"], mesh.shape["rhs"]),
        mesh=mesh,
        in_specs=(
            P(None, ("site", "rhs"), None),
            P(None, ("site", "rhs"), None),
            P(),
            P("site", None, None, None),
            P("site", None),
            P(),
        ),
        out_specs=(P("rhs", "site", None), P("rhs", "site", None)),
        check_vma=False,
    )
```

```python
import functools

import jax
import jax.numpy as jnp
from jax import lax
from jax.experimental import pallas as pl
from jax.experimental.pallas import tpu as pltpu
from jax.sharding import PartitionSpec as P

MESH = pl.DeviceIdType.MESH
MR_STEPS = 2


def extended_2(array, sides, width):
    for axis, dim in sides:
        size, length = (lax.axis_size(axis), array.shape[dim])
        up = [(i, (i + 1) % size) for i in range(size)]
        down = [(j, i) for i, j in up]
        last = lax.slice_in_dim(array, length - width, length, axis=dim)
        first = lax.slice_in_dim(array, 0, width, axis=dim)
        before = lax.ppermute(last, axis, up)
        after = lax.ppermute(first, axis, down)
        array = jnp.concatenate([before, array, after], axis=dim)
    return array


def turned(vectors):
    half_width = vectors.shape[-1] // 2
    return jnp.concatenate([-vectors[..., half_width:], vectors[..., :half_width]], axis=-1)


def conj_turned(vectors):
    half_width = vectors.shape[-1] // 2
    return jnp.concatenate([vectors[..., half_width:], -vectors[..., :half_width]], axis=-1)


def scaled(alpha_re, alpha_im, vectors):
    return alpha_re[:, None, None] * vectors + alpha_im[:, None, None] * turned(vectors)


def small_solve(coarse_inverse, coef_re, coef_im):
    highest = lax.Precision.HIGHEST
    real_part = coarse_inverse[0]
    imag_part = coarse_inverse[1]
    solved_re = jnp.dot(
        real_part, coef_re, precision=highest, preferred_element_type=jnp.float32
    ) - jnp.dot(imag_part, coef_im, precision=highest, preferred_element_type=jnp.float32)
    solved_im = jnp.dot(
        real_part, coef_im, precision=highest, preferred_element_type=jnp.float32
    ) + jnp.dot(imag_part, coef_re, precision=highest, preferred_element_type=jnp.float32)
    return (solved_re, solved_im)


def operate(vectors, coupling, neighbours):
    slots = vectors.shape[0]
    sites_here = vectors.shape[1]
    width = vectors.shape[2]
    reach = sites_here // 2
    extended = extended_2(vectors, (("site", 1),), reach)
    anchor = lax.axis_index("site") * sites_here
    total = sites_here * lax.axis_size("site")
    position = (neighbours - anchor + reach) % total
    beside = jnp.take(extended, position.reshape(-1), axis=1).reshape(slots, sites_here, 8, width)
    stacked = jnp.concatenate([vectors[:, :, None, :], beside], axis=2).reshape(
        slots, sites_here, 9 * width
    )
    blocks = coupling.reshape(sites_here, 9 * width, width)
    product = lax.dot_general(
        stacked, blocks, (((2,), (1,)), ((1,), (0,))), preferred_element_type=jnp.float32
    )
    return jnp.transpose(product, (1, 0, 2))


def staged(rhs_vecs, deflation, coarse_inverse, coupling, neighbours, grouping):
    ordered = jnp.take(rhs_vecs, grouping, axis=0)
    coef_re = jnp.einsum("ksc,rsc->kr", deflation, ordered, preferred_element_type=jnp.float32)
    coef_im = jnp.einsum(
        "ksc,rsc->kr", deflation, conj_turned(ordered), preferred_element_type=jnp.float32
    )
    group_re, group_im = (
        lax.psum_scatter(coef_re, "rhs", scatter_dimension=1, tiled=True),
        lax.psum_scatter(coef_im, "rhs", scatter_dimension=1, tiled=True),
    )
    group_re, group_im = lax.psum((group_re, group_im), "site")
    share_re, share_im = small_solve(coarse_inverse, group_re, group_im)
    solved_re, solved_im = (
        lax.all_gather(share_re.astype(jnp.bfloat16), "rhs", axis=1, tiled=True).astype(
            share_re.dtype
        ),
        lax.all_gather(share_im.astype(jnp.bfloat16), "rhs", axis=1, tiled=True).astype(
            share_im.dtype
        ),
    )
    low_re = solved_re.astype(jnp.bfloat16)
    low_im = solved_im.astype(jnp.bfloat16)
    start = jnp.einsum("kr,ksc->rsc", low_re, deflation, preferred_element_type=jnp.float32)
    start = start + jnp.einsum(
        "kr,ksc->rsc", low_im, turned(deflation), preferred_element_type=jnp.float32
    )
    start_low = start.astype(jnp.bfloat16)
    given_low, placed = (
        lax.all_to_all(ordered, "rhs", split_axis=0, concat_axis=1, tiled=True),
        lax.all_to_all(start_low, "rhs", split_axis=0, concat_axis=1, tiled=True),
    )
    given = given_low.astype(jnp.float32)
    solution = placed.astype(jnp.float32)
    residual = given - operate(placed, coupling, neighbours)
    for iteration in range(MR_STEPS):
        image = operate(residual.astype(jnp.bfloat16), coupling, neighbours)
        upper_re = jnp.sum(image * residual, axis=(1, 2))
        upper_im = jnp.sum(image * conj_turned(residual), axis=(1, 2))
        lower = jnp.sum(image * image, axis=(1, 2))
        upper_re, upper_im, lower = lax.psum((upper_re, upper_im, lower), "site")
        alpha_re = upper_re / lower
        alpha_im = upper_im / lower
        solution = solution + scaled(alpha_re, alpha_im, residual)
        residual = residual - scaled(alpha_re, alpha_im, image)
    return (solution, residual)


def lanes_turned(values, conj):
    width = values.shape[-1]
    lane = lax.broadcasted_iota(jnp.int32, values.shape, values.ndim - 1)
    rolled = pltpu.roll(values, width // 2, values.ndim - 1)
    low = lane < width // 2
    if conj:
        return jnp.where(low, rolled, -rolled)
    return jnp.where(low, -rolled, rolled)


def fused_kernel(
    n_site, n_rhs,
    rhs_hbm, defl_hbm, inv_hbm, coup_hbm, nb_hbm, group_ref,
    sol_ref, res_ref,
    rhs_ref, defl_ref, wide, inv, nb, coup, gathered, ordered, given, coef, parts, solved, solved_all, ext0, ext1, ext2, image, sums, sums_all,
    rhs_sem, defl_sem, inv_sem, nb_sem, coup_sem, coef_send, coef_recv, pack_send, pack_recv, defl_send, defl_recv,
    solved_send, solved_recv, halo_send, halo_recv, sums_send, sums_recv,
):
    devices = n_site * n_rhs
    width = rhs_ref.shape[1]
    slots = group_ref.shape[1]
    sites_local = rhs_ref.shape[0] // slots
    sites_here = coup_hbm.shape[0]
    reach = sites_here // 2
    group = slots // n_rhs
    share = group // n_site
    vecs = inv_hbm.shape[1]
    f32, bf16 = jnp.float32, jnp.bfloat16
    exts = (ext0, ext1, ext2)

    my_site = lax.axis_index("site")
    my_rhs = lax.axis_index("rhs")
    me = my_rhs * n_site + my_site

    def peer(d):
        at = lax.rem(me + d, devices)
        return at, (lax.rem(at, n_site), at // n_site)

    load_coup = pltpu.make_async_copy(coup_hbm, coup, coup_sem)
    load_nb = pltpu.make_async_copy(nb_hbm, nb, nb_sem)
    load_inv = pltpu.make_async_copy(inv_hbm, inv, inv_sem)
    load_rhs = pltpu.make_async_copy(rhs_hbm, rhs_ref, rhs_sem)
    load_defl = pltpu.make_async_copy(defl_hbm, defl_ref, defl_sem)
    load_defl.start()
    load_rhs.start()
    load_nb.start()
    load_inv.start()
    load_coup.start()
    barrier = pltpu.get_barrier_semaphore()

    def greet(d, carry):
        _, dev = peer(d)
        pl.semaphore_signal(barrier, inc=1, device_id=dev, device_id_type=MESH)
        return carry

    lax.fori_loop(1, devices, greet, 0)
    own = my_rhs * sites_local
    load_defl.wait()
    wide[...] = defl_ref[...].astype(f32)
    basis = []
    for i in range(sites_local):
        block = wide[pl.ds(i, vecs, stride=sites_local), :].astype(bf16)
        gathered[own + i] = block
        basis.append(block)
    basis = jnp.concatenate(basis, axis=1)

    row = lax.broadcasted_iota(jnp.int32, (slots * sites_local, slots), 0)
    wanted = group_ref[...] * sites_local
    tn = (((0,), (0,)), ((), ()))
    row2 = lax.broadcasted_iota(jnp.int32, (2 * slots, slots), 0)
    col2 = lax.broadcasted_iota(jnp.int32, (2 * slots, slots), 1)
    spread = jnp.where(col2 == (row2 // (2 * share)) * share + row2 % share, 1.0, 0.0).astype(bf16)
    part = (lax.broadcasted_iota(jnp.int32, (2 * slots, width), 0) // share) % 2
    both = []
    load_rhs.wait()
    for i in range(sites_local):
        placed = jnp.where(row == wanted + i, 1.0, 0.0).astype(bf16)
        g = lax.dot_general(placed, rhs_ref[...], tn, preferred_element_type=f32).astype(bf16)
        ordered[i] = g
        two = jnp.dot(spread, g, preferred_element_type=f32)
        both.append(jnp.where(part == 1, lanes_turned(two, True), two).astype(bf16))
    both = jnp.concatenate(both, axis=1)
    total = lax.dot_general(both, basis, (((1,), (1,)), ((), ())), preferred_element_type=f32)
    coef[...] = total.reshape(devices, 2 * share, vecs).astype(bf16)

    pl.semaphore_wait(barrier, devices - 1)

    def coef_copy(d):
        at, dev = peer(d)
        return pltpu.make_async_remote_copy(
            src_ref=coef.at[at], dst_ref=parts.at[me], send_sem=coef_send.at[d],
            recv_sem=coef_recv.at[me], device_id=dev, device_id_type=MESH)

    def coef_start(d, carry):
        coef_copy(d).start()
        return carry

    lax.fori_loop(1, devices, coef_start, 0)

    packs, defls = [], []
    for d in range(1, n_rhs):
        other = lax.rem(my_rhs + d, n_rhs)
        packs.append(pltpu.make_async_remote_copy(
            src_ref=ordered.at[:, pl.ds(pl.multiple_of(other * group, group), group), :],
            dst_ref=given.at[pl.ds(own, sites_local)],
            send_sem=pack_send.at[d], recv_sem=pack_recv.at[d],
            device_id=(my_site, other), device_id_type=MESH))
        defls.append(pltpu.make_async_remote_copy(
            src_ref=gathered.at[pl.ds(own, sites_local)],
            dst_ref=gathered.at[pl.ds(own, sites_local)],
            send_sem=defl_send.at[d], recv_sem=defl_recv.at[d],
            device_id=(my_site, other), device_id_type=MESH))
    for copy in packs + defls:
        copy.start()
    given[pl.ds(own, sites_local)] = ordered[:, pl.ds(pl.multiple_of(my_rhs * group, group), group), :]
    parts[me] = coef[me]

    def coef_wait(d, carry):
        at, dev = peer(d)
        pltpu.make_async_remote_copy(
            src_ref=coef.at[at], dst_ref=parts.at[at], send_sem=coef_send.at[d],
            recv_sem=coef_recv.at[at], device_id=dev, device_id_type=MESH).wait_recv()
        return carry

    lax.fori_loop(1, devices, coef_wait, 0)
    mine = jnp.sum(parts[...].astype(f32), axis=0)
    load_inv.wait()
    swapped = pltpu.roll(mine, share, 0)
    first = lax.broadcasted_iota(jnp.int32, mine.shape, 0) < share
    swapped = jnp.where(first, -swapped, swapped)
    nt = (((1,), (1,)), ((), ()))
    out = lax.dot_general(mine, inv[0], nt, precision=lax.Precision.HIGHEST, preferred_element_type=f32)
    out = out + lax.dot_general(swapped, inv[1], nt, precision=lax.Precision.HIGHEST, preferred_element_type=f32)
    solved[...] = out.astype(bf16)

    def along(d):
        return lax.rem(my_site + d, n_site)

    def to_all_sites(src, dst, send, recv):
        copies = []
        for d in range(1, n_site):
            copies.append(pltpu.make_async_remote_copy(
                src_ref=src, dst_ref=dst.at[my_site], send_sem=send.at[d],
                recv_sem=recv.at[d], device_id=(along(d), my_rhs), device_id_type=MESH))
        for copy in copies:
            copy.start()
        dst[my_site] = src[...]
        return copies

    copies = to_all_sites(solved, solved_all, solved_send, solved_recv)

    def coef_sent(d, carry):
        coef_copy(d).wait_send()
        return carry

    lax.fori_loop(1, devices, coef_sent, 0)
    row3 = lax.broadcasted_iota(jnp.int32, (2 * group, 2 * group), 0)
    col3 = lax.broadcasted_iota(jnp.int32, (2 * group, 2 * group), 1)
    slot3 = row3 % group
    want = (slot3 // share) * (2 * share) + (row3 // group) * share + slot3 % share
    sort = jnp.where(col3 == want, 1.0, 0.0).astype(bf16)
    for copy in copies:
        copy.wait()
    low = solved_all[...].astype(f32).reshape(2 * group, vecs).astype(bf16)
    low = jnp.dot(sort, low, preferred_element_type=f32).astype(bf16)
    for copy in packs + defls:
        copy.wait()
    for i in range(sites_here):
        z = jnp.dot(low, gathered[i], preferred_element_type=f32)
        start = (z[:group] + lanes_turned(z[group:], False)).astype(bf16)
        ext0[reach + i] = start
        sol_ref[i] = start.astype(f32)

    def halo(step):
        buf = exts[step]
        up = pltpu.make_async_remote_copy(
            src_ref=buf.at[pl.ds(sites_here, reach)], dst_ref=buf.at[pl.ds(0, reach)],
            send_sem=halo_send.at[2 * step], recv_sem=halo_recv.at[2 * step],
            device_id=(along(1), my_rhs), device_id_type=MESH)
        down = pltpu.make_async_remote_copy(
            src_ref=buf.at[pl.ds(reach, reach)], dst_ref=buf.at[pl.ds(reach + sites_here, reach)],
            send_sem=halo_send.at[2 * step + 1], recv_sem=halo_recv.at[2 * step + 1],
            device_id=(along(n_site - 1), my_rhs), device_id_type=MESH)
        up.start()
        down.start()
        return up, down

    anchor = my_site * sites_here - reach

    def operate(step, i):
        pieces = [exts[step][reach + i]]
        for m in range(nb.shape[0]):
            at = (nb[m, i] - anchor) & (2 * sites_here - 1)
            pieces.append(exts[step][at])
        stacked = jnp.concatenate(pieces, axis=1)
        return jnp.dot(stacked, coup[i], preferred_element_type=f32)

    copies = halo(0)
    load_nb.wait()
    load_coup.wait()
    for copy in copies:
        copy.wait()
    for i in range(sites_here):
        r = given[i].astype(f32) - operate(0, i)
        res_ref[i] = r
        ext1[reach + i] = r.astype(bf16)

    lane = lax.broadcasted_iota(jnp.int32, (8, width), 1)
    bands = group // 8
    for step in range(2):
        for copy in halo(step + 1):
            copy.wait()
        tops = [jnp.zeros((group, width), f32) for _ in range(3)]
        for i in range(sites_here):
            y = operate(step + 1, i)
            r = res_ref[i]
            image[i] = y
            tops[0] = tops[0] + y * r
            tops[1] = tops[1] + y * lanes_turned(r, True)
            tops[2] = tops[2] + y * y
        tile = jnp.zeros((8, width), f32)
        for v in range(3):
            column = jnp.sum(tops[v], axis=1, keepdims=True)
            for b in range(bands):
                tile = jnp.where(lane == 3 * b + v, column[8 * b:8 * b + 8], tile)
        sums[step] = tile
        for copy in to_all_sites(sums.at[step], sums_all.at[step], sums_send.at[step], sums_recv.at[step]):
            copy.wait()
        tile = jnp.sum(sums_all[step], axis=0)
        values = []
        for v in range(3):
            values.append(jnp.concatenate([tile[:, 3 * b + v:3 * b + v + 1] for b in range(bands)], axis=0))
        alpha_re = values[0] / values[2]
        alpha_im = values[1] / values[2]
        for i in range(sites_here):
            r, y = res_ref[i], image[i]
            sol_ref[i] = sol_ref[i] + (alpha_re * r + alpha_im * lanes_turned(r, False))
            r = r - (alpha_re * y + alpha_im * lanes_turned(y, False))
            res_ref[i] = r
            if step == 0:
                ext2[reach + i] = r.astype(bf16)


def fused(n_site, n_rhs, rhs_vecs, deflation, coarse_inverse, coupling, neighbours, grouping):
    f32, bf16 = jnp.float32, jnp.bfloat16
    slots, sites_local, width = rhs_vecs.shape
    vecs = deflation.shape[0]
    sites_here = coupling.shape[0]
    group = slots // n_rhs
    share = group // n_site
    devices = n_site * n_rhs
    blocks = coupling.reshape(sites_here, -1, width)
    vmem = pl.BlockSpec(memory_space=pltpu.VMEM)
    hbm = pl.BlockSpec(memory_space=pltpu.HBM)
    out = jax.ShapeDtypeStruct((sites_here, group, width), f32)
    dma = pltpu.SemaphoreType.DMA
    sol, res = pl.pallas_call(
        functools.partial(fused_kernel, n_site, n_rhs),
        out_shape=(out, out),
        in_specs=[hbm, hbm, hbm, hbm, hbm, vmem],
        out_specs=(vmem, vmem),
        scratch_shapes=[
            pltpu.VMEM((slots * sites_local, width), bf16),
            pltpu.VMEM((vecs * sites_local, width), bf16),
            pltpu.VMEM((vecs * sites_local, width), f32),
            pltpu.VMEM(coarse_inverse.shape, f32),
            pltpu.SMEM(neighbours.shape[::-1], jnp.int32),
            pltpu.VMEM(blocks.shape, bf16),
            pltpu.VMEM((sites_here, vecs, width), bf16),
            pltpu.VMEM((sites_local, slots, width), bf16),
            pltpu.VMEM((sites_here, group, width), bf16),
            pltpu.VMEM((devices, 2 * share, vecs), bf16),
            pltpu.VMEM((devices, 2 * share, vecs), bf16),
            pltpu.VMEM((2 * share, vecs), bf16),
            pltpu.VMEM((n_site, 2 * share, vecs), bf16),
            pltpu.VMEM((2 * sites_here, group, width), bf16),
            pltpu.VMEM((2 * sites_here, group, width), bf16),
            pltpu.VMEM((2 * sites_here, group, width), bf16),
            pltpu.VMEM((sites_here, group, width), f32),
            pltpu.VMEM((2, 8, width), f32),
            pltpu.VMEM((2, n_site, 8, width), f32),
            dma, dma, dma, dma, dma, dma((devices,)), dma((devices,)), dma((n_rhs,)), dma((n_rhs,)),
            dma((n_rhs,)), dma((n_rhs,)), dma((n_site,)), dma((n_site,)),
            dma((6,)), dma((6,)), dma((2, n_site)), dma((2, n_site)),
        ],
        compiler_params=pltpu.CompilerParams(
            collective_id=0, has_side_effects=True, vmem_limit_bytes=63 * 1024 * 1024),
    )(
        rhs_vecs.reshape(slots * sites_local, width),
        deflation.reshape(vecs * sites_local, width),
        coarse_inverse,
        blocks,
        neighbours.T,
        grouping.reshape(1, slots),
    )
    return jnp.transpose(sol, (1, 0, 2)), jnp.transpose(res, (1, 0, 2))


def fits(n_site, n_rhs, rhs_vecs, coupling):
    slots, sites_local, width = rhs_vecs.shape
    sites_here = coupling.shape[0]
    group = slots // n_rhs
    share = group // n_site
    return (
        share * n_site * n_rhs == slots
        and (2 * share) % 8 == 0
        and group % 16 == 0
        and 3 * (group // 8) <= width
        and slots % 128 == 0
        and width % 128 == 0
        and sites_local * n_rhs == sites_here
        and n_site >= 3
        and n_site % 2 == 0
        and sites_here & (sites_here - 1) == 0
    )


def per_device(n_site, n_rhs, *arrays):
    if fits(n_site, n_rhs, arrays[0], arrays[3]):
        return fused(n_site, n_rhs, *arrays)
    return staged(*arrays)


def solution(mesh):
    return jax.shard_map(
        functools.partial(per_device, mesh.shape["site"], mesh.shape["rhs"]),
        mesh=mesh,
        in_specs=(
            P(None, ("site", "rhs"), None),
            P(None, ("site", "rhs"), None),
            P(),
            P("site", None, None, None),
            P("site", None),
            P(),
        ),
        out_specs=(P("rhs", "site", None), P("rhs", "site", None)),
        check_vma=False,
    )
```

```python
import functools

import jax
import jax.numpy as jnp
from jax import lax
from jax.experimental import pallas as pl
from jax.experimental.pallas import tpu as pltpu
from jax.sharding import PartitionSpec as P

MESH = pl.DeviceIdType.MESH
MR_STEPS = 2


def extended_2(array, sides, width):
    for axis, dim in sides:
        size, length = (lax.axis_size(axis), array.shape[dim])
        up = [(i, (i + 1) % size) for i in range(size)]
        down = [(j, i) for i, j in up]
        last = lax.slice_in_dim(array, length - width, length, axis=dim)
        first = lax.slice_in_dim(array, 0, width, axis=dim)
        before = lax.ppermute(last, axis, up)
        after = lax.ppermute(first, axis, down)
        array = jnp.concatenate([before, array, after], axis=dim)
    return array


def turned(vectors):
    half_width = vectors.shape[-1] // 2
    return jnp.concatenate([-vectors[..., half_width:], vectors[..., :half_width]], axis=-1)


def conj_turned(vectors):
    half_width = vectors.shape[-1] // 2
    return jnp.concatenate([vectors[..., half_width:], -vectors[..., :half_width]], axis=-1)


def scaled(alpha_re, alpha_im, vectors):
    return alpha_re[:, None, None] * vectors + alpha_im[:, None, None] * turned(vectors)


def small_solve(coarse_inverse, coef_re, coef_im):
    highest = lax.Precision.HIGHEST
    real_part = coarse_inverse[0]
    imag_part = coarse_inverse[1]
    solved_re = jnp.dot(
        real_part, coef_re, precision=highest, preferred_element_type=jnp.float32
    ) - jnp.dot(imag_part, coef_im, precision=highest, preferred_element_type=jnp.float32)
    solved_im = jnp.dot(
        real_part, coef_im, precision=highest, preferred_element_type=jnp.float32
    ) + jnp.dot(imag_part, coef_re, precision=highest, preferred_element_type=jnp.float32)
    return (solved_re, solved_im)


def operate(vectors, coupling, neighbours):
    slots = vectors.shape[0]
    sites_here = vectors.shape[1]
    width = vectors.shape[2]
    reach = sites_here // 2
    extended = extended_2(vectors, (("site", 1),), reach)
    anchor = lax.axis_index("site") * sites_here
    total = sites_here * lax.axis_size("site")
    position = (neighbours - anchor + reach) % total
    beside = jnp.take(extended, position.reshape(-1), axis=1).reshape(slots, sites_here, 8, width)
    stacked = jnp.concatenate([vectors[:, :, None, :], beside], axis=2).reshape(
        slots, sites_here, 9 * width
    )
    blocks = coupling.reshape(sites_here, 9 * width, width)
    product = lax.dot_general(
        stacked, blocks, (((2,), (1,)), ((1,), (0,))), preferred_element_type=jnp.float32
    )
    return jnp.transpose(product, (1, 0, 2))


def staged(rhs_vecs, deflation, coarse_inverse, coupling, neighbours, grouping):
    ordered = jnp.take(rhs_vecs, grouping, axis=0)
    coef_re = jnp.einsum("ksc,rsc->kr", deflation, ordered, preferred_element_type=jnp.float32)
    coef_im = jnp.einsum(
        "ksc,rsc->kr", deflation, conj_turned(ordered), preferred_element_type=jnp.float32
    )
    group_re, group_im = (
        lax.psum_scatter(coef_re, "rhs", scatter_dimension=1, tiled=True),
        lax.psum_scatter(coef_im, "rhs", scatter_dimension=1, tiled=True),
    )
    group_re, group_im = lax.psum((group_re, group_im), "site")
    share_re, share_im = small_solve(coarse_inverse, group_re, group_im)
    solved_re, solved_im = (
        lax.all_gather(share_re.astype(jnp.bfloat16), "rhs", axis=1, tiled=True).astype(
            share_re.dtype
        ),
        lax.all_gather(share_im.astype(jnp.bfloat16), "rhs", axis=1, tiled=True).astype(
            share_im.dtype
        ),
    )
    low_re = solved_re.astype(jnp.bfloat16)
    low_im = solved_im.astype(jnp.bfloat16)
    start = jnp.einsum("kr,ksc->rsc", low_re, deflation, preferred_element_type=jnp.float32)
    start = start + jnp.einsum(
        "kr,ksc->rsc", low_im, turned(deflation), preferred_element_type=jnp.float32
    )
    start_low = start.astype(jnp.bfloat16)
    given_low, placed = (
        lax.all_to_all(ordered, "rhs", split_axis=0, concat_axis=1, tiled=True),
        lax.all_to_all(start_low, "rhs", split_axis=0, concat_axis=1, tiled=True),
    )
    given = given_low.astype(jnp.float32)
    solution = placed.astype(jnp.float32)
    residual = given - operate(placed, coupling, neighbours)
    for iteration in range(MR_STEPS):
        image = operate(residual.astype(jnp.bfloat16), coupling, neighbours)
        upper_re = jnp.sum(image * residual, axis=(1, 2))
        upper_im = jnp.sum(image * conj_turned(residual), axis=(1, 2))
        lower = jnp.sum(image * image, axis=(1, 2))
        upper_re, upper_im, lower = lax.psum((upper_re, upper_im, lower), "site")
        alpha_re = upper_re / lower
        alpha_im = upper_im / lower
        solution = solution + scaled(alpha_re, alpha_im, residual)
        residual = residual - scaled(alpha_re, alpha_im, image)
    return (solution, residual)


def lanes_turned(values, conj):
    width = values.shape[-1]
    lane = lax.broadcasted_iota(jnp.int32, values.shape, values.ndim - 1)
    rolled = pltpu.roll(values, width // 2, values.ndim - 1)
    low = lane < width // 2
    if conj:
        return jnp.where(low, rolled, -rolled)
    return jnp.where(low, -rolled, rolled)


def fused_kernel(
    n_site, n_rhs,
    rhs_hbm, defl_hbm, inv_hbm, coup_hbm, nb_hbm, group_ref,
    sol_ref, res_ref,
    rhs_ref, defl_ref, wide, inv, nb, coup, gathered, ordered, given, coef, parts, solved, solved_all, low0, high0, low1, high1, low2, high2, low3, high3, first_res, image, sums, sums_all,
    rhs_sem, defl_sem, inv_sem, nb_sem, coup_sem, coef_send, coef_recv, pack_send, pack_recv, defl_send, defl_recv,
    solved_send, solved_recv, halo_send, halo_recv, sums_send, sums_recv,
):
    devices = n_site * n_rhs
    width = rhs_ref.shape[1]
    slots = group_ref.shape[1]
    sites_local = rhs_ref.shape[0] // slots
    sites_here = coup_hbm.shape[0]
    reach = sites_here // 2
    group = slots // n_rhs
    share = group // n_site
    vecs = inv_hbm.shape[1]
    f32, bf16 = jnp.float32, jnp.bfloat16
    bufs = ((low0, high0), (low1, high1), (low2, high2), (low3, high3))

    my_site = lax.axis_index("site")
    my_rhs = lax.axis_index("rhs")
    me = my_rhs * n_site + my_site

    def peer(d):
        at = lax.rem(me + d, devices)
        return at, (lax.rem(at, n_site), at // n_site)

    load_coup = pltpu.make_async_copy(coup_hbm, coup, coup_sem)
    load_nb = pltpu.make_async_copy(nb_hbm, nb, nb_sem)
    load_inv = pltpu.make_async_copy(inv_hbm, inv, inv_sem)
    load_rhs = pltpu.make_async_copy(rhs_hbm, rhs_ref, rhs_sem)
    load_defl = pltpu.make_async_copy(defl_hbm, defl_ref, defl_sem)
    load_defl.start()
    load_rhs.start()
    load_nb.start()
    load_inv.start()
    load_coup.start()
    barrier = pltpu.get_barrier_semaphore()

    def greet(d, carry):
        _, dev = peer(d)
        pl.semaphore_signal(barrier, inc=1, device_id=dev, device_id_type=MESH)
        return carry

    lax.fori_loop(1, devices, greet, 0)
    own = my_rhs * sites_local
    load_defl.wait()
    wide[...] = defl_ref[...].astype(f32)
    basis = []
    for i in range(sites_local):
        block = wide[pl.ds(i, vecs, stride=sites_local), :].astype(bf16)
        gathered[own + i] = block
        basis.append(block)
    basis = jnp.concatenate(basis, axis=1)

    row = lax.broadcasted_iota(jnp.int32, (slots * sites_local, slots), 0)
    wanted = group_ref[...] * sites_local
    tn = (((0,), (0,)), ((), ()))
    row2 = lax.broadcasted_iota(jnp.int32, (2 * slots, slots), 0)
    col2 = lax.broadcasted_iota(jnp.int32, (2 * slots, slots), 1)
    spread = jnp.where(col2 == (row2 // (2 * share)) * share + row2 % share, 1.0, 0.0).astype(bf16)
    part = (lax.broadcasted_iota(jnp.int32, (2 * slots, width), 0) // share) % 2
    both = []
    load_rhs.wait()
    for i in range(sites_local):
        placed = jnp.where(row == wanted + i, 1.0, 0.0).astype(bf16)
        g = lax.dot_general(placed, rhs_ref[...], tn, preferred_element_type=f32).astype(bf16)
        ordered[i] = g
        two = jnp.dot(spread, g, preferred_element_type=f32)
        both.append(jnp.where(part == 1, lanes_turned(two, True), two).astype(bf16))
    both = jnp.concatenate(both, axis=1)
    total = lax.dot_general(both, basis, (((1,), (1,)), ((), ())), preferred_element_type=f32)
    coef[...] = total.reshape(devices, 2 * share, vecs).astype(bf16)

    pl.semaphore_wait(barrier, devices - 1)

    def coef_copy(d):
        at, dev = peer(d)
        return pltpu.make_async_remote_copy(
            src_ref=coef.at[at], dst_ref=parts.at[me], send_sem=coef_send.at[d],
            recv_sem=coef_recv.at[me], device_id=dev, device_id_type=MESH)

    def coef_start(d, carry):
        coef_copy(d).start()
        return carry

    lax.fori_loop(1, devices, coef_start, 0)

    packs, defls = [], []
    for d in range(1, n_rhs):
        other = lax.rem(my_rhs + d, n_rhs)
        packs.append(pltpu.make_async_remote_copy(
            src_ref=ordered.at[:, pl.ds(pl.multiple_of(other * group, group), group), :],
            dst_ref=given.at[pl.ds(own, sites_local)],
            send_sem=pack_send.at[d], recv_sem=pack_recv.at[d],
            device_id=(my_site, other), device_id_type=MESH))
        defls.append(pltpu.make_async_remote_copy(
            src_ref=gathered.at[pl.ds(own, sites_local)],
            dst_ref=gathered.at[pl.ds(own, sites_local)],
            send_sem=defl_send.at[d], recv_sem=defl_recv.at[d],
            device_id=(my_site, other), device_id_type=MESH))
    for copy in packs + defls:
        copy.start()
    given[pl.ds(own, sites_local)] = ordered[:, pl.ds(pl.multiple_of(my_rhs * group, group), group), :]
    parts[me] = coef[me]

    def coef_wait(d, carry):
        at, dev = peer(d)
        pltpu.make_async_remote_copy(
            src_ref=coef.at[at], dst_ref=parts.at[at], send_sem=coef_send.at[d],
            recv_sem=coef_recv.at[at], device_id=dev, device_id_type=MESH).wait_recv()
        return carry

    lax.fori_loop(1, devices, coef_wait, 0)
    mine = jnp.sum(parts[...].astype(f32), axis=0)
    load_inv.wait()
    swapped = pltpu.roll(mine, share, 0)
    first = lax.broadcasted_iota(jnp.int32, mine.shape, 0) < share
    swapped = jnp.where(first, -swapped, swapped)
    nt = (((1,), (1,)), ((), ()))
    out = lax.dot_general(mine, inv[0], nt, precision=lax.Precision.HIGHEST, preferred_element_type=f32)
    out = out + lax.dot_general(swapped, inv[1], nt, precision=lax.Precision.HIGHEST, preferred_element_type=f32)
    solved[...] = out.astype(bf16)

    def along(d):
        return lax.rem(my_site + d, n_site)

    def to_all_sites(src, dst, send, recv):
        copies = []
        for d in range(1, n_site):
            copies.append(pltpu.make_async_remote_copy(
                src_ref=src, dst_ref=dst.at[my_site], send_sem=send.at[d],
                recv_sem=recv.at[d], device_id=(along(d), my_rhs), device_id_type=MESH))
        for copy in copies:
            copy.start()
        dst[my_site] = src[...]
        return copies

    copies = to_all_sites(solved, solved_all, solved_send, solved_recv)

    def coef_sent(d, carry):
        coef_copy(d).wait_send()
        return carry

    lax.fori_loop(1, devices, coef_sent, 0)
    row3 = lax.broadcasted_iota(jnp.int32, (2 * group, 2 * group), 0)
    col3 = lax.broadcasted_iota(jnp.int32, (2 * group, 2 * group), 1)
    slot3 = row3 % group
    want = (slot3 // share) * (2 * share) + (row3 // group) * share + slot3 % share
    sort = jnp.where(col3 == want, 1.0, 0.0).astype(bf16)
    for copy in copies:
        copy.wait()
    low = solved_all[...].astype(f32).reshape(2 * group, vecs).astype(bf16)
    low = jnp.dot(sort, low, preferred_element_type=f32).astype(bf16)
    for copy in packs + defls:
        copy.wait()
    anchor = my_site * sites_here - reach
    halves = (range(reach), range(reach, sites_here))

    def keep(step, i, values):
        for buf in bufs[step]:
            buf[reach + i] = values

    def halo(step, half):
        own_buf, out_buf = bufs[step]
        if half == 0:
            source, target, to = out_buf.at[pl.ds(reach, reach)], out_buf.at[pl.ds(reach + sites_here, reach)], n_site - 1
        else:
            source, target, to = own_buf.at[pl.ds(sites_here, reach)], own_buf.at[pl.ds(0, reach)], 1
        copy = pltpu.make_async_remote_copy(
            src_ref=source, dst_ref=target,
            send_sem=halo_send.at[2 * step + half], recv_sem=halo_recv.at[2 * step + half],
            device_id=(along(to), my_rhs), device_id_type=MESH)
        copy.start()
        return copy

    def operate(step, i):
        buf = bufs[step][i // reach]
        pieces = [buf[reach + i]]
        for m in range(nb.shape[0]):
            pieces.append(buf[(nb[m, i] - anchor) & (2 * sites_here - 1)])
        stacked = jnp.concatenate(pieces, axis=1)
        return jnp.dot(stacked, coup[i], preferred_element_type=f32)

    copies = []
    for half in (0, 1):
        for i in halves[half]:
            z = jnp.dot(low, gathered[i], preferred_element_type=f32)
            start = (z[:group] + lanes_turned(z[group:], False)).astype(bf16)
            keep(0, i, start)
            sol_ref[i] = start.astype(f32)
        copies.append(halo(0, half))
    load_nb.wait()
    load_coup.wait()
    later = [None, None]
    for half in (1, 0):
        copies[1 - half].wait_recv()
        for i in halves[half]:
            r = given[i].astype(f32) - operate(0, i)
            first_res[i] = r
            keep(1, i, r.astype(bf16))
        later[half] = halo(1, half)
    sent = copies + later

    lane = lax.broadcasted_iota(jnp.int32, (8, width), 1)
    bands = group // 8

    def apply(step, half, held, into, tops, low_too):
        for i in halves[half]:
            y = operate(step, i)
            r = held[i]
            into[i] = y
            if low_too:
                keep(2, i, y.astype(bf16))
            tops[0] = tops[0] + y * r
            tops[1] = tops[1] + y * lanes_turned(r, True)
            tops[2] = tops[2] + y * y

    def send_sums(step, tops):
        tile = jnp.zeros((8, width), f32)
        for v in range(3):
            column = jnp.sum(tops[v], axis=1, keepdims=True)
            for b in range(bands):
                tile = jnp.where(lane == 3 * b + v, column[8 * b:8 * b + 8], tile)
        sums[step] = tile
        return to_all_sites(sums.at[step], sums_all.at[step], sums_send.at[step], sums_recv.at[step])

    def alphas(step, waits):
        for copy in waits:
            copy.wait()
        tile = jnp.sum(sums_all[step], axis=0)
        values = []
        for v in range(3):
            values.append(jnp.concatenate([tile[:, 3 * b + v:3 * b + v + 1] for b in range(bands)], axis=0))
        alpha_re = jnp.broadcast_to(values[0] / values[2], (group, width))
        alpha_im = jnp.broadcast_to(values[1] / values[2], (group, width))
        return lambda vectors: alpha_re * vectors + alpha_im * lanes_turned(vectors, False)

    tops = [jnp.zeros((group, width), f32) for _ in range(3)]
    beside = []
    for half in (0, 1):
        later[1 - half].wait_recv()
        apply(1, half, first_res, image, tops, True)
        if half == 0:
            beside.append(halo(2, 0))
    waits = send_sums(0, tops)
    beside.append(halo(2, 1))
    first_scaled = alphas(0, waits)
    for i in range(sites_here):
        r = first_res[i] - first_scaled(image[i])
        res_ref[i] = r
        keep(3, i, r.astype(bf16))
    for half in (1, 0):
        beside[1 - half].wait_recv()
        at = (0, reach + sites_here)[half]
        for i in range(reach):
            r = bufs[1][half][at + i].astype(f32) - first_scaled(bufs[2][half][at + i].astype(f32))
            bufs[3][half][at + i] = r.astype(bf16)
    tops = [jnp.zeros((group, width), f32) for _ in range(3)]
    for half in (1, 0):
        apply(3, half, res_ref, image, tops, False)
    waits = send_sums(1, tops)
    for i in range(sites_here):
        sol_ref[i] = sol_ref[i] + first_scaled(first_res[i])
    for copy in sent + beside:
        copy.wait_send()
    second_scaled = alphas(1, waits)
    for i in range(sites_here):
        r = res_ref[i]
        sol_ref[i] = sol_ref[i] + second_scaled(r)
        res_ref[i] = r - second_scaled(image[i])


def fused(n_site, n_rhs, rhs_vecs, deflation, coarse_inverse, coupling, neighbours, grouping):
    f32, bf16 = jnp.float32, jnp.bfloat16
    slots, sites_local, width = rhs_vecs.shape
    vecs = deflation.shape[0]
    sites_here = coupling.shape[0]
    group = slots // n_rhs
    share = group // n_site
    devices = n_site * n_rhs
    blocks = coupling.reshape(sites_here, -1, width)
    vmem = pl.BlockSpec(memory_space=pltpu.VMEM)
    hbm = pl.BlockSpec(memory_space=pltpu.HBM)
    out = jax.ShapeDtypeStruct((sites_here, group, width), f32)
    dma = pltpu.SemaphoreType.DMA
    sol, res = pl.pallas_call(
        functools.partial(fused_kernel, n_site, n_rhs),
        out_shape=(out, out),
        in_specs=[hbm, hbm, hbm, hbm, hbm, vmem],
        out_specs=(vmem, vmem),
        scratch_shapes=[
            pltpu.VMEM((slots * sites_local, width), bf16),
            pltpu.VMEM((vecs * sites_local, width), bf16),
            pltpu.VMEM((vecs * sites_local, width), f32),
            pltpu.VMEM(coarse_inverse.shape, f32),
            pltpu.SMEM(neighbours.shape[::-1], jnp.int32),
            pltpu.VMEM(blocks.shape, bf16),
            pltpu.VMEM((sites_here, vecs, width), bf16),
            pltpu.VMEM((sites_local, slots, width), bf16),
            pltpu.VMEM((sites_here, group, width), bf16),
            pltpu.VMEM((devices, 2 * share, vecs), bf16),
            pltpu.VMEM((devices, 2 * share, vecs), bf16),
            pltpu.VMEM((2 * share, vecs), bf16),
            pltpu.VMEM((n_site, 2 * share, vecs), bf16),
            pltpu.VMEM((2 * sites_here, group, width), bf16),
            pltpu.VMEM((2 * sites_here, group, width), bf16),
            pltpu.VMEM((2 * sites_here, group, width), bf16),
            pltpu.VMEM((2 * sites_here, group, width), bf16),
            pltpu.VMEM((2 * sites_here, group, width), bf16),
            pltpu.VMEM((2 * sites_here, group, width), bf16),
            pltpu.VMEM((2 * sites_here, group, width), bf16),
            pltpu.VMEM((2 * sites_here, group, width), bf16),
            pltpu.VMEM((sites_here, group, width), f32),
            pltpu.VMEM((sites_here, group, width), f32),
            pltpu.VMEM((2, 8, width), f32),
            pltpu.VMEM((2, n_site, 8, width), f32),
            dma, dma, dma, dma, dma, dma((devices,)), dma((devices,)), dma((n_rhs,)), dma((n_rhs,)),
            dma((n_rhs,)), dma((n_rhs,)), dma((n_site,)), dma((n_site,)),
            dma((6,)), dma((6,)), dma((2, n_site)), dma((2, n_site)),
        ],
        compiler_params=pltpu.CompilerParams(
            collective_id=0, has_side_effects=True, vmem_limit_bytes=63 * 1024 * 1024),
    )(
        rhs_vecs.reshape(slots * sites_local, width),
        deflation.reshape(vecs * sites_local, width),
        coarse_inverse,
        blocks,
        neighbours.T,
        grouping.reshape(1, slots),
    )
    return jnp.transpose(sol, (1, 0, 2)), jnp.transpose(res, (1, 0, 2))


def fits(n_site, n_rhs, rhs_vecs, coupling):
    slots, sites_local, width = rhs_vecs.shape
    sites_here = coupling.shape[0]
    group = slots // n_rhs
    share = group // n_site
    return (
        share * n_site * n_rhs == slots
        and (2 * share) % 8 == 0
        and group % 16 == 0
        and 3 * (group // 8) <= width
        and slots % 128 == 0
        and width % 128 == 0
        and sites_local * n_rhs == sites_here
        and n_site >= 3
        and n_site % 2 == 0
        and sites_here & (sites_here - 1) == 0
    )


def per_device(n_site, n_rhs, *arrays):
    if fits(n_site, n_rhs, arrays[0], arrays[3]):
        return fused(n_site, n_rhs, *arrays)
    return staged(*arrays)


def solution(mesh):
    return jax.shard_map(
        functools.partial(per_device, mesh.shape["site"], mesh.shape["rhs"]),
        mesh=mesh,
        in_specs=(
            P(None, ("site", "rhs"), None),
            P(None, ("site", "rhs"), None),
            P(),
            P("site", None, None, None),
            P("site", None),
            P(),
        ),
        out_specs=(P("rhs", "site", None), P("rhs", "site", None)),
        check_vma=False,
    )
```

```python
import functools

import jax
import jax.numpy as jnp
from jax import lax
from jax.experimental import pallas as pl
from jax.experimental.pallas import tpu as pltpu
from jax.sharding import PartitionSpec as P

MESH = pl.DeviceIdType.MESH
MR_STEPS = 2


def extended_2(array, sides, width):
    for axis, dim in sides:
        size, length = (lax.axis_size(axis), array.shape[dim])
        up = [(i, (i + 1) % size) for i in range(size)]
        down = [(j, i) for i, j in up]
        last = lax.slice_in_dim(array, length - width, length, axis=dim)
        first = lax.slice_in_dim(array, 0, width, axis=dim)
        before = lax.ppermute(last, axis, up)
        after = lax.ppermute(first, axis, down)
        array = jnp.concatenate([before, array, after], axis=dim)
    return array


def turned(vectors):
    half_width = vectors.shape[-1] // 2
    return jnp.concatenate([-vectors[..., half_width:], vectors[..., :half_width]], axis=-1)


def conj_turned(vectors):
    half_width = vectors.shape[-1] // 2
    return jnp.concatenate([vectors[..., half_width:], -vectors[..., :half_width]], axis=-1)


def scaled(alpha_re, alpha_im, vectors):
    return alpha_re[:, None, None] * vectors + alpha_im[:, None, None] * turned(vectors)


def small_solve(coarse_inverse, coef_re, coef_im):
    highest = lax.Precision.HIGHEST
    real_part = coarse_inverse[0]
    imag_part = coarse_inverse[1]
    solved_re = jnp.dot(
        real_part, coef_re, precision=highest, preferred_element_type=jnp.float32
    ) - jnp.dot(imag_part, coef_im, precision=highest, preferred_element_type=jnp.float32)
    solved_im = jnp.dot(
        real_part, coef_im, precision=highest, preferred_element_type=jnp.float32
    ) + jnp.dot(imag_part, coef_re, precision=highest, preferred_element_type=jnp.float32)
    return (solved_re, solved_im)


def operate(vectors, coupling, neighbours):
    slots = vectors.shape[0]
    sites_here = vectors.shape[1]
    width = vectors.shape[2]
    reach = sites_here // 2
    extended = extended_2(vectors, (("site", 1),), reach)
    anchor = lax.axis_index("site") * sites_here
    total = sites_here * lax.axis_size("site")
    position = (neighbours - anchor + reach) % total
    beside = jnp.take(extended, position.reshape(-1), axis=1).reshape(slots, sites_here, 8, width)
    stacked = jnp.concatenate([vectors[:, :, None, :], beside], axis=2).reshape(
        slots, sites_here, 9 * width
    )
    blocks = coupling.reshape(sites_here, 9 * width, width)
    product = lax.dot_general(
        stacked, blocks, (((2,), (1,)), ((1,), (0,))), preferred_element_type=jnp.float32
    )
    return jnp.transpose(product, (1, 0, 2))


def staged(rhs_vecs, deflation, coarse_inverse, coupling, neighbours, grouping):
    ordered = jnp.take(rhs_vecs, grouping, axis=0)
    coef_re = jnp.einsum("ksc,rsc->kr", deflation, ordered, preferred_element_type=jnp.float32)
    coef_im = jnp.einsum(
        "ksc,rsc->kr", deflation, conj_turned(ordered), preferred_element_type=jnp.float32
    )
    group_re, group_im = (
        lax.psum_scatter(coef_re, "rhs", scatter_dimension=1, tiled=True),
        lax.psum_scatter(coef_im, "rhs", scatter_dimension=1, tiled=True),
    )
    group_re, group_im = lax.psum((group_re, group_im), "site")
    share_re, share_im = small_solve(coarse_inverse, group_re, group_im)
    solved_re, solved_im = (
        lax.all_gather(share_re.astype(jnp.bfloat16), "rhs", axis=1, tiled=True).astype(
            share_re.dtype
        ),
        lax.all_gather(share_im.astype(jnp.bfloat16), "rhs", axis=1, tiled=True).astype(
            share_im.dtype
        ),
    )
    low_re = solved_re.astype(jnp.bfloat16)
    low_im = solved_im.astype(jnp.bfloat16)
    start = jnp.einsum("kr,ksc->rsc", low_re, deflation, preferred_element_type=jnp.float32)
    start = start + jnp.einsum(
        "kr,ksc->rsc", low_im, turned(deflation), preferred_element_type=jnp.float32
    )
    start_low = start.astype(jnp.bfloat16)
    given_low, placed = (
        lax.all_to_all(ordered, "rhs", split_axis=0, concat_axis=1, tiled=True),
        lax.all_to_all(start_low, "rhs", split_axis=0, concat_axis=1, tiled=True),
    )
    given = given_low.astype(jnp.float32)
    solution = placed.astype(jnp.float32)
    residual = given - operate(placed, coupling, neighbours)
    for iteration in range(MR_STEPS):
        image = operate(residual.astype(jnp.bfloat16), coupling, neighbours)
        upper_re = jnp.sum(image * residual, axis=(1, 2))
        upper_im = jnp.sum(image * conj_turned(residual), axis=(1, 2))
        lower = jnp.sum(image * image, axis=(1, 2))
        upper_re, upper_im, lower = lax.psum((upper_re, upper_im, lower), "site")
        alpha_re = upper_re / lower
        alpha_im = upper_im / lower
        solution = solution + scaled(alpha_re, alpha_im, residual)
        residual = residual - scaled(alpha_re, alpha_im, image)
    return (solution, residual)


def lanes_turned(values, conj):
    width = values.shape[-1]
    lane = lax.broadcasted_iota(jnp.int32, values.shape, values.ndim - 1)
    rolled = pltpu.roll(values, width // 2, values.ndim - 1)
    low = lane < width // 2
    if conj:
        return jnp.where(low, rolled, -rolled)
    return jnp.where(low, -rolled, rolled)


def fused_kernel(
    n_site, n_rhs,
    rhs_hbm, defl_hbm, inv_hbm, coup_hbm, nb_hbm, group_ref,
    sol_ref, res_ref,
    rhs_ref, defl_ref, wide, inv, nb, coup, gathered, ordered, given, coef, parts, solved, solved_all, low0, high0, low1, high1, low2, high2, low3, high3, first_res, image, sums, sums_all,
    rhs_sem, defl_sem, inv_sem, nb_sem, coup_sem, coef_send, coef_recv, pack_send, pack_recv, defl_send, defl_recv,
    solved_send, solved_recv, halo_send, halo_recv, sums_send, sums_recv,
):
    devices = n_site * n_rhs
    width = rhs_ref.shape[1]
    slots = group_ref.shape[1]
    sites_local = rhs_ref.shape[0] // slots
    sites_here = coup_hbm.shape[0]
    reach = sites_here // 2
    group = slots // n_rhs
    share = group // n_site
    vecs = inv_hbm.shape[1]
    f32, bf16 = jnp.float32, jnp.bfloat16
    bufs = ((low0, high0), (low1, high1), (low2, high2), (low3, high3))

    my_site = lax.axis_index("site")
    my_rhs = lax.axis_index("rhs")
    me = my_rhs * n_site + my_site

    def peer(d):
        at = lax.rem(me + d, devices)
        return at, (lax.rem(at, n_site), at // n_site)

    load_coup = pltpu.make_async_copy(coup_hbm, coup, coup_sem)
    load_nb = pltpu.make_async_copy(nb_hbm, nb, nb_sem)
    load_inv = pltpu.make_async_copy(inv_hbm, inv, inv_sem)
    load_rhs = pltpu.make_async_copy(rhs_hbm, rhs_ref, rhs_sem)
    load_defl = pltpu.make_async_copy(defl_hbm, defl_ref, defl_sem)
    load_defl.start()
    load_rhs.start()
    load_nb.start()
    load_inv.start()
    load_coup.start()
    barrier = pltpu.get_barrier_semaphore()

    def greet(d, carry):
        _, dev = peer(d)
        pl.semaphore_signal(barrier, inc=1, device_id=dev, device_id_type=MESH)
        return carry

    lax.fori_loop(1, devices, greet, 0)
    own = my_rhs * sites_local
    load_defl.wait()
    wide[...] = defl_ref[...].astype(f32)
    basis = []
    for i in range(sites_local):
        block = wide[pl.ds(i, vecs, stride=sites_local), :].astype(bf16)
        gathered[own + i] = block
        basis.append(block)
    basis = jnp.concatenate(basis, axis=1)

    row = lax.broadcasted_iota(jnp.int32, (slots * sites_local, slots), 0)
    wanted = group_ref[...] * sites_local
    tn = (((0,), (0,)), ((), ()))
    row2 = lax.broadcasted_iota(jnp.int32, (2 * slots, slots), 0)
    col2 = lax.broadcasted_iota(jnp.int32, (2 * slots, slots), 1)
    spread = jnp.where(col2 == (row2 // (2 * share)) * share + row2 % share, 1.0, 0.0).astype(bf16)
    part = (lax.broadcasted_iota(jnp.int32, (2 * slots, width), 0) // share) % 2
    both = []
    load_rhs.wait()
    for i in range(sites_local):
        placed = jnp.where(row == wanted + i, 1.0, 0.0).astype(bf16)
        g = lax.dot_general(placed, rhs_ref[...], tn, preferred_element_type=f32).astype(bf16)
        ordered[i] = g
        two = jnp.dot(spread, g, preferred_element_type=f32)
        both.append(jnp.where(part == 1, lanes_turned(two, True), two).astype(bf16))
    both = jnp.concatenate(both, axis=1)
    total = lax.dot_general(both, basis, (((1,), (1,)), ((), ())), preferred_element_type=f32)
    coef[...] = total.reshape(devices, 2 * share, vecs).astype(bf16)

    pl.semaphore_wait(barrier, devices - 1)

    def coef_copy(d):
        at, dev = peer(d)
        return pltpu.make_async_remote_copy(
            src_ref=coef.at[at], dst_ref=parts.at[me], send_sem=coef_send.at[d],
            recv_sem=coef_recv.at[me], device_id=dev, device_id_type=MESH)

    def coef_start(d, carry):
        coef_copy(d).start()
        return carry

    lax.fori_loop(1, devices, coef_start, 0)

    def to_rhs(source, target, other, sends, recvs, d):
        return pltpu.make_async_remote_copy(
            src_ref=source, dst_ref=target, send_sem=sends.at[d], recv_sem=recvs.at[d],
            device_id=(my_site, other), device_id_type=MESH)

    half = n_rhs // 2
    twin = my_rhs + 1 - 2 * lax.rem(my_rhs, 2)
    mine_at = gathered.at[pl.ds(own, sites_local)]
    packs, defls = [], []
    for d in range(1, n_rhs):
        other = lax.rem(my_rhs + d, n_rhs)
        packs.append(to_rhs(
            ordered.at[:, pl.ds(pl.multiple_of(other * group, group), group), :],
            given.at[pl.ds(own, sites_local)], other, pack_send, pack_recv, d))
    defls.append(to_rhs(mine_at, mine_at, twin, defl_send, defl_recv, 0))
    relays = []
    for d in range(1, half):
        other = lax.rem(my_rhs + 2 * d, n_rhs)
        defls.append(to_rhs(mine_at, mine_at, other, defl_send, defl_recv, d))
        came = lax.rem(my_rhs + n_rhs - 2 * d, n_rhs) * sites_local
        block = gathered.at[pl.ds(came, sites_local)]
        relays.append(to_rhs(block, block, twin, defl_send, defl_recv, half + d))
    for copy in packs + defls:
        copy.start()
    given[pl.ds(own, sites_local)] = ordered[:, pl.ds(pl.multiple_of(my_rhs * group, group), group), :]
    parts[me] = coef[me]

    def coef_wait(d, carry):
        at, dev = peer(d)
        pltpu.make_async_remote_copy(
            src_ref=coef.at[at], dst_ref=parts.at[at], send_sem=coef_send.at[d],
            recv_sem=coef_recv.at[at], device_id=dev, device_id_type=MESH).wait_recv()
        return carry

    lax.fori_loop(1, devices, coef_wait, 0)
    mine = jnp.sum(parts[...].astype(f32), axis=0)
    load_inv.wait()
    swapped = pltpu.roll(mine, share, 0)
    first = lax.broadcasted_iota(jnp.int32, mine.shape, 0) < share
    swapped = jnp.where(first, -swapped, swapped)
    nt = (((1,), (1,)), ((), ()))
    out = lax.dot_general(mine, inv[0], nt, precision=lax.Precision.HIGHEST, preferred_element_type=f32)
    out = out + lax.dot_general(swapped, inv[1], nt, precision=lax.Precision.HIGHEST, preferred_element_type=f32)
    solved[...] = out.astype(bf16)

    def along(d):
        return lax.rem(my_site + d, n_site)

    def to_all_sites(src, dst, send, recv):
        copies = []
        for d in range(1, n_site):
            copies.append(pltpu.make_async_remote_copy(
                src_ref=src, dst_ref=dst.at[my_site], send_sem=send.at[d],
                recv_sem=recv.at[d], device_id=(along(d), my_rhs), device_id_type=MESH))
        for copy in copies:
            copy.start()
        dst[my_site] = src[...]
        return copies

    copies = to_all_sites(solved, solved_all, solved_send, solved_recv)
    for copy, relay in zip(defls[1:], relays):
        copy.wait_recv()
        relay.start()

    def coef_sent(d, carry):
        coef_copy(d).wait_send()
        return carry

    lax.fori_loop(1, devices, coef_sent, 0)
    row3 = lax.broadcasted_iota(jnp.int32, (2 * group, 2 * group), 0)
    col3 = lax.broadcasted_iota(jnp.int32, (2 * group, 2 * group), 1)
    slot3 = row3 % group
    want = (slot3 // share) * (2 * share) + (row3 // group) * share + slot3 % share
    sort = jnp.where(col3 == want, 1.0, 0.0).astype(bf16)
    for copy in copies:
        copy.wait()
    low = solved_all[...].astype(f32).reshape(2 * group, vecs).astype(bf16)
    low = jnp.dot(sort, low, preferred_element_type=f32).astype(bf16)
    for copy in packs + defls[:1] + relays:
        copy.wait()
    for copy in defls[1:]:
        copy.wait_send()
    anchor = my_site * sites_here - reach
    halves = (range(reach), range(reach, sites_here))

    def keep(step, i, values):
        for buf in bufs[step]:
            buf[reach + i] = values

    def halo(step, half):
        own_buf, out_buf = bufs[step]
        if half == 0:
            source, target, to = out_buf.at[pl.ds(reach, reach)], out_buf.at[pl.ds(reach + sites_here, reach)], n_site - 1
        else:
            source, target, to = own_buf.at[pl.ds(sites_here, reach)], own_buf.at[pl.ds(0, reach)], 1
        copy = pltpu.make_async_remote_copy(
            src_ref=source, dst_ref=target,
            send_sem=halo_send.at[2 * step + half], recv_sem=halo_recv.at[2 * step + half],
            device_id=(along(to), my_rhs), device_id_type=MESH)
        copy.start()
        return copy

    def operate(step, i):
        buf = bufs[step][i // reach]
        pieces = [buf[reach + i]]
        for m in range(nb.shape[0]):
            pieces.append(buf[(nb[m, i] - anchor) & (2 * sites_here - 1)])
        stacked = jnp.concatenate(pieces, axis=1)
        return jnp.dot(stacked, coup[i], preferred_element_type=f32)

    copies = []
    for half in (0, 1):
        for i in halves[half]:
            z = jnp.dot(low, gathered[i], preferred_element_type=f32)
            start = (z[:group] + lanes_turned(z[group:], False)).astype(bf16)
            keep(0, i, start)
            sol_ref[i] = start.astype(f32)
        copies.append(halo(0, half))
    load_nb.wait()
    load_coup.wait()
    later = [None, None]
    for half in (1, 0):
        copies[1 - half].wait_recv()
        for i in halves[half]:
            r = given[i].astype(f32) - operate(0, i)
            first_res[i] = r
            keep(1, i, r.astype(bf16))
        later[half] = halo(1, half)
    sent = copies + later

    lane = lax.broadcasted_iota(jnp.int32, (8, width), 1)
    bands = group // 8

    def apply(step, half, held, into, tops, low_too):
        for i in halves[half]:
            y = operate(step, i)
            r = held[i]
            into[i] = y
            if low_too:
                keep(2, i, y.astype(bf16))
            tops[0] = tops[0] + y * r
            tops[1] = tops[1] + y * lanes_turned(r, True)
            tops[2] = tops[2] + y * y

    def send_sums(step, tops):
        tile = jnp.zeros((8, width), f32)
        for v in range(3):
            column = jnp.sum(tops[v], axis=1, keepdims=True)
            for b in range(bands):
                tile = jnp.where(lane == 3 * b + v, column[8 * b:8 * b + 8], tile)
        sums[step] = tile
        return to_all_sites(sums.at[step], sums_all.at[step], sums_send.at[step], sums_recv.at[step])

    def alphas(step, waits):
        for copy in waits:
            copy.wait()
        tile = jnp.sum(sums_all[step], axis=0)
        values = []
        for v in range(3):
            values.append(jnp.concatenate([tile[:, 3 * b + v:3 * b + v + 1] for b in range(bands)], axis=0))
        alpha_re = jnp.broadcast_to(values[0] / values[2], (group, width))
        alpha_im = jnp.broadcast_to(values[1] / values[2], (group, width))
        return lambda vectors: alpha_re * vectors + alpha_im * lanes_turned(vectors, False)

    tops = [jnp.zeros((group, width), f32) for _ in range(3)]
    beside = []
    for half in (0, 1):
        later[1 - half].wait_recv()
        apply(1, half, first_res, image, tops, True)
        if half == 0:
            beside.append(halo(2, 0))
    waits = send_sums(0, tops)
    beside.append(halo(2, 1))
    first_scaled = alphas(0, waits)
    for i in range(sites_here):
        r = first_res[i] - first_scaled(image[i])
        res_ref[i] = r
        keep(3, i, r.astype(bf16))
    for half in (1, 0):
        beside[1 - half].wait_recv()
        at = (0, reach + sites_here)[half]
        for i in range(reach):
            r = bufs[1][half][at + i].astype(f32) - first_scaled(bufs[2][half][at + i].astype(f32))
            bufs[3][half][at + i] = r.astype(bf16)
    tops = [jnp.zeros((group, width), f32) for _ in range(3)]
    for half in (1, 0):
        apply(3, half, res_ref, image, tops, False)
    waits = send_sums(1, tops)
    for i in range(sites_here):
        sol_ref[i] = sol_ref[i] + first_scaled(first_res[i])
    for copy in sent + beside:
        copy.wait_send()
    second_scaled = alphas(1, waits)
    for i in range(sites_here):
        r = res_ref[i]
        sol_ref[i] = sol_ref[i] + second_scaled(r)
        res_ref[i] = r - second_scaled(image[i])


def fused(n_site, n_rhs, rhs_vecs, deflation, coarse_inverse, coupling, neighbours, grouping):
    f32, bf16 = jnp.float32, jnp.bfloat16
    slots, sites_local, width = rhs_vecs.shape
    vecs = deflation.shape[0]
    sites_here = coupling.shape[0]
    group = slots // n_rhs
    share = group // n_site
    devices = n_site * n_rhs
    blocks = coupling.reshape(sites_here, -1, width)
    vmem = pl.BlockSpec(memory_space=pltpu.VMEM)
    hbm = pl.BlockSpec(memory_space=pltpu.HBM)
    out = jax.ShapeDtypeStruct((sites_here, group, width), f32)
    dma = pltpu.SemaphoreType.DMA
    sol, res = pl.pallas_call(
        functools.partial(fused_kernel, n_site, n_rhs),
        out_shape=(out, out),
        in_specs=[hbm, hbm, hbm, hbm, hbm, vmem],
        out_specs=(vmem, vmem),
        scratch_shapes=[
            pltpu.VMEM((slots * sites_local, width), bf16),
            pltpu.VMEM((vecs * sites_local, width), bf16),
            pltpu.VMEM((vecs * sites_local, width), f32),
            pltpu.VMEM(coarse_inverse.shape, f32),
            pltpu.SMEM(neighbours.shape[::-1], jnp.int32),
            pltpu.VMEM(blocks.shape, bf16),
            pltpu.VMEM((sites_here, vecs, width), bf16),
            pltpu.VMEM((sites_local, slots, width), bf16),
            pltpu.VMEM((sites_here, group, width), bf16),
            pltpu.VMEM((devices, 2 * share, vecs), bf16),
            pltpu.VMEM((devices, 2 * share, vecs), bf16),
            pltpu.VMEM((2 * share, vecs), bf16),
            pltpu.VMEM((n_site, 2 * share, vecs), bf16),
            pltpu.VMEM((2 * sites_here, group, width), bf16),
            pltpu.VMEM((2 * sites_here, group, width), bf16),
            pltpu.VMEM((2 * sites_here, group, width), bf16),
            pltpu.VMEM((2 * sites_here, group, width), bf16),
            pltpu.VMEM((2 * sites_here, group, width), bf16),
            pltpu.VMEM((2 * sites_here, group, width), bf16),
            pltpu.VMEM((2 * sites_here, group, width), bf16),
            pltpu.VMEM((2 * sites_here, group, width), bf16),
            pltpu.VMEM((sites_here, group, width), f32),
            pltpu.VMEM((sites_here, group, width), f32),
            pltpu.VMEM((2, 8, width), f32),
            pltpu.VMEM((2, n_site, 8, width), f32),
            dma, dma, dma, dma, dma, dma((devices,)), dma((devices,)), dma((n_rhs,)), dma((n_rhs,)),
            dma((n_rhs,)), dma((n_rhs,)), dma((n_site,)), dma((n_site,)),
            dma((6,)), dma((6,)), dma((2, n_site)), dma((2, n_site)),
        ],
        compiler_params=pltpu.CompilerParams(
            collective_id=0, has_side_effects=True, vmem_limit_bytes=63 * 1024 * 1024),
    )(
        rhs_vecs.reshape(slots * sites_local, width),
        deflation.reshape(vecs * sites_local, width),
        coarse_inverse,
        blocks,
        neighbours.T,
        grouping.reshape(1, slots),
    )
    return jnp.transpose(sol, (1, 0, 2)), jnp.transpose(res, (1, 0, 2))


def fits(n_site, n_rhs, rhs_vecs, coupling):
    slots, sites_local, width = rhs_vecs.shape
    sites_here = coupling.shape[0]
    group = slots // n_rhs
    share = group // n_site
    return (
        share * n_site * n_rhs == slots
        and (2 * share) % 8 == 0
        and group % 16 == 0
        and 3 * (group // 8) <= width
        and slots % 128 == 0
        and width % 128 == 0
        and sites_local * n_rhs == sites_here
        and n_site >= 3
        and n_rhs % 2 == 0
        and n_site % 2 == 0
        and sites_here & (sites_here - 1) == 0
    )


def per_device(n_site, n_rhs, *arrays):
    if fits(n_site, n_rhs, arrays[0], arrays[3]):
        return fused(n_site, n_rhs, *arrays)
    return staged(*arrays)


def solution(mesh):
    return jax.shard_map(
        functools.partial(per_device, mesh.shape["site"], mesh.shape["rhs"]),
        mesh=mesh,
        in_specs=(
            P(None, ("site", "rhs"), None),
            P(None, ("site", "rhs"), None),
            P(),
            P("site", None, None, None),
            P("site", None),
            P(),
        ),
        out_specs=(P("rhs", "site", None), P("rhs", "site", None)),
        check_vma=False,
    )
```

```python
import functools

import jax
import jax.numpy as jnp
from jax import lax
from jax.experimental import pallas as pl
from jax.experimental.pallas import tpu as pltpu
from jax.sharding import PartitionSpec as P

MESH = pl.DeviceIdType.MESH
MR_STEPS = 2


def extended_2(array, sides, width):
    for axis, dim in sides:
        size, length = (lax.axis_size(axis), array.shape[dim])
        up = [(i, (i + 1) % size) for i in range(size)]
        down = [(j, i) for i, j in up]
        last = lax.slice_in_dim(array, length - width, length, axis=dim)
        first = lax.slice_in_dim(array, 0, width, axis=dim)
        before = lax.ppermute(last, axis, up)
        after = lax.ppermute(first, axis, down)
        array = jnp.concatenate([before, array, after], axis=dim)
    return array


def turned(vectors):
    half_width = vectors.shape[-1] // 2
    return jnp.concatenate([-vectors[..., half_width:], vectors[..., :half_width]], axis=-1)


def conj_turned(vectors):
    half_width = vectors.shape[-1] // 2
    return jnp.concatenate([vectors[..., half_width:], -vectors[..., :half_width]], axis=-1)


def scaled(alpha_re, alpha_im, vectors):
    return alpha_re[:, None, None] * vectors + alpha_im[:, None, None] * turned(vectors)


def small_solve(coarse_inverse, coef_re, coef_im):
    highest = lax.Precision.HIGHEST
    real_part = coarse_inverse[0]
    imag_part = coarse_inverse[1]
    solved_re = jnp.dot(
        real_part, coef_re, precision=highest, preferred_element_type=jnp.float32
    ) - jnp.dot(imag_part, coef_im, precision=highest, preferred_element_type=jnp.float32)
    solved_im = jnp.dot(
        real_part, coef_im, precision=highest, preferred_element_type=jnp.float32
    ) + jnp.dot(imag_part, coef_re, precision=highest, preferred_element_type=jnp.float32)
    return (solved_re, solved_im)


def operate(vectors, coupling, neighbours):
    slots = vectors.shape[0]
    sites_here = vectors.shape[1]
    width = vectors.shape[2]
    reach = sites_here // 2
    extended = extended_2(vectors, (("site", 1),), reach)
    anchor = lax.axis_index("site") * sites_here
    total = sites_here * lax.axis_size("site")
    position = (neighbours - anchor + reach) % total
    beside = jnp.take(extended, position.reshape(-1), axis=1).reshape(slots, sites_here, 8, width)
    stacked = jnp.concatenate([vectors[:, :, None, :], beside], axis=2).reshape(
        slots, sites_here, 9 * width
    )
    blocks = coupling.reshape(sites_here, 9 * width, width)
    product = lax.dot_general(
        stacked, blocks, (((2,), (1,)), ((1,), (0,))), preferred_element_type=jnp.float32
    )
    return jnp.transpose(product, (1, 0, 2))


def staged(rhs_vecs, deflation, coarse_inverse, coupling, neighbours, grouping):
    ordered = jnp.take(rhs_vecs, grouping, axis=0)
    coef_re = jnp.einsum("ksc,rsc->kr", deflation, ordered, preferred_element_type=jnp.float32)
    coef_im = jnp.einsum(
        "ksc,rsc->kr", deflation, conj_turned(ordered), preferred_element_type=jnp.float32
    )
    group_re, group_im = (
        lax.psum_scatter(coef_re, "rhs", scatter_dimension=1, tiled=True),
        lax.psum_scatter(coef_im, "rhs", scatter_dimension=1, tiled=True),
    )
    group_re, group_im = lax.psum((group_re, group_im), "site")
    share_re, share_im = small_solve(coarse_inverse, group_re, group_im)
    solved_re, solved_im = (
        lax.all_gather(share_re.astype(jnp.bfloat16), "rhs", axis=1, tiled=True).astype(
            share_re.dtype
        ),
        lax.all_gather(share_im.astype(jnp.bfloat16), "rhs", axis=1, tiled=True).astype(
            share_im.dtype
        ),
    )
    low_re = solved_re.astype(jnp.bfloat16)
    low_im = solved_im.astype(jnp.bfloat16)
    start = jnp.einsum("kr,ksc->rsc", low_re, deflation, preferred_element_type=jnp.float32)
    start = start + jnp.einsum(
        "kr,ksc->rsc", low_im, turned(deflation), preferred_element_type=jnp.float32
    )
    start_low = start.astype(jnp.bfloat16)
    given_low, placed = (
        lax.all_to_all(ordered, "rhs", split_axis=0, concat_axis=1, tiled=True),
        lax.all_to_all(start_low, "rhs", split_axis=0, concat_axis=1, tiled=True),
    )
    given = given_low.astype(jnp.float32)
    solution = placed.astype(jnp.float32)
    residual = given - operate(placed, coupling, neighbours)
    for iteration in range(MR_STEPS):
        image = operate(residual.astype(jnp.bfloat16), coupling, neighbours)
        upper_re = jnp.sum(image * residual, axis=(1, 2))
        upper_im = jnp.sum(image * conj_turned(residual), axis=(1, 2))
        lower = jnp.sum(image * image, axis=(1, 2))
        upper_re, upper_im, lower = lax.psum((upper_re, upper_im, lower), "site")
        alpha_re = upper_re / lower
        alpha_im = upper_im / lower
        solution = solution + scaled(alpha_re, alpha_im, residual)
        residual = residual - scaled(alpha_re, alpha_im, image)
    return (solution, residual)


def lanes_turned(values, conj):
    width = values.shape[-1]
    lane = lax.broadcasted_iota(jnp.int32, values.shape, values.ndim - 1)
    rolled = pltpu.roll(values, width // 2, values.ndim - 1)
    low = lane < width // 2
    if conj:
        return jnp.where(low, rolled, -rolled)
    return jnp.where(low, -rolled, rolled)


def fused_kernel(
    n_site, n_rhs,
    rhs_hbm, defl_hbm, inv_hbm, coup_hbm, nb_hbm, group_ref,
    sol_out, res_out,
    sol_ref, res_ref, rhs_ref, defl_ref, wide, inv, nb, coup, gathered, ordered, given, coef, parts, solved, solved_all, low0, high0, low1, high1, low2, high2, low3, high3, first_res, image, sums, sums_all,
    rhs_sem, defl_sem, inv_sem, nb_sem, coup_sem, coef_send, coef_recv, pack_send, pack_recv, defl_send, defl_recv,
    solved_send, solved_recv, halo_send, halo_recv, sums_send, sums_recv,
):
    devices = n_site * n_rhs
    width = rhs_ref.shape[1]
    slots = group_ref.shape[1]
    sites_local = rhs_ref.shape[0] // slots
    sites_here = coup_hbm.shape[0]
    reach = sites_here // 2
    group = slots // n_rhs
    share = group // n_site
    vecs = inv_hbm.shape[1]
    f32, bf16 = jnp.float32, jnp.bfloat16
    bufs = ((low0, high0), (low1, high1), (low2, high2), (low3, high3))

    my_site = lax.axis_index("site")
    my_rhs = lax.axis_index("rhs")
    me = my_rhs * n_site + my_site

    def peer(d):
        at = lax.rem(me + d, devices)
        return at, (lax.rem(at, n_site), at // n_site)

    load_coup = pltpu.make_async_copy(coup_hbm, coup, coup_sem)
    load_nb = pltpu.make_async_copy(nb_hbm, nb, nb_sem)
    load_inv = pltpu.make_async_copy(inv_hbm, inv, inv_sem)
    load_rhs = pltpu.make_async_copy(rhs_hbm, rhs_ref, rhs_sem)
    load_defl = pltpu.make_async_copy(defl_hbm, defl_ref, defl_sem)
    load_defl.start()
    load_rhs.start()
    load_nb.start()
    load_inv.start()
    load_coup.start()
    barrier = pltpu.get_barrier_semaphore()

    def greet(d, carry):
        _, dev = peer(d)
        pl.semaphore_signal(barrier, inc=1, device_id=dev, device_id_type=MESH)
        return carry

    lax.fori_loop(1, devices, greet, 0)
    own = my_rhs * sites_local
    load_defl.wait()
    wide[...] = defl_ref[...].astype(f32)
    basis = []
    for i in range(sites_local):
        block = wide[pl.ds(i, vecs, stride=sites_local), :].astype(bf16)
        gathered[own + i] = block
        basis.append(block)
    basis = jnp.concatenate(basis, axis=1)

    row = lax.broadcasted_iota(jnp.int32, (slots * sites_local, slots), 0)
    wanted = group_ref[...] * sites_local
    tn = (((0,), (0,)), ((), ()))
    row2 = lax.broadcasted_iota(jnp.int32, (2 * slots, slots), 0)
    col2 = lax.broadcasted_iota(jnp.int32, (2 * slots, slots), 1)
    spread = jnp.where(col2 == (row2 // (2 * share)) * share + row2 % share, 1.0, 0.0).astype(bf16)
    part = (lax.broadcasted_iota(jnp.int32, (2 * slots, width), 0) // share) % 2
    both = []
    load_rhs.wait()
    for i in range(sites_local):
        placed = jnp.where(row == wanted + i, 1.0, 0.0).astype(bf16)
        g = lax.dot_general(placed, rhs_ref[...], tn, preferred_element_type=f32).astype(bf16)
        ordered[i] = g
        two = jnp.dot(spread, g, preferred_element_type=f32)
        both.append(jnp.where(part == 1, lanes_turned(two, True), two).astype(bf16))
    both = jnp.concatenate(both, axis=1)
    total = lax.dot_general(both, basis, (((1,), (1,)), ((), ())), preferred_element_type=f32)
    coef[...] = total.reshape(devices, 2 * share, vecs).astype(bf16)

    pl.semaphore_wait(barrier, devices - 1)

    def coef_copy(d):
        at, dev = peer(d)
        return pltpu.make_async_remote_copy(
            src_ref=coef.at[at], dst_ref=parts.at[me], send_sem=coef_send.at[d],
            recv_sem=coef_recv.at[me], device_id=dev, device_id_type=MESH)

    def coef_start(d, carry):
        coef_copy(d).start()
        return carry

    lax.fori_loop(1, devices, coef_start, 0)

    def to_rhs(source, target, other, sends, recvs, d):
        return pltpu.make_async_remote_copy(
            src_ref=source, dst_ref=target, send_sem=sends.at[d], recv_sem=recvs.at[d],
            device_id=(my_site, other), device_id_type=MESH)

    half = n_rhs // 2
    twin = my_rhs + 1 - 2 * lax.rem(my_rhs, 2)
    mine_at = gathered.at[pl.ds(own, sites_local)]
    packs, defls = [], []
    for d in range(1, n_rhs):
        other = lax.rem(my_rhs + d, n_rhs)
        packs.append(to_rhs(
            ordered.at[:, pl.ds(pl.multiple_of(other * group, group), group), :],
            given.at[pl.ds(own, sites_local)], other, pack_send, pack_recv, d))
    defls.append(to_rhs(mine_at, mine_at, twin, defl_send, defl_recv, 0))
    relays = []
    for d in range(1, half):
        other = lax.rem(my_rhs + 2 * d, n_rhs)
        defls.append(to_rhs(mine_at, mine_at, other, defl_send, defl_recv, d))
        came = lax.rem(my_rhs + n_rhs - 2 * d, n_rhs) * sites_local
        block = gathered.at[pl.ds(came, sites_local)]
        relays.append(to_rhs(block, block, twin, defl_send, defl_recv, half + d))
    for copy in packs + defls:
        copy.start()
    given[pl.ds(own, sites_local)] = ordered[:, pl.ds(pl.multiple_of(my_rhs * group, group), group), :]
    parts[me] = coef[me]

    def coef_wait(d, carry):
        at, dev = peer(d)
        pltpu.make_async_remote_copy(
            src_ref=coef.at[at], dst_ref=parts.at[at], send_sem=coef_send.at[d],
            recv_sem=coef_recv.at[at], device_id=dev, device_id_type=MESH).wait_recv()
        return carry

    lax.fori_loop(1, devices, coef_wait, 0)
    mine = jnp.sum(parts[...].astype(f32), axis=0)
    load_inv.wait()
    swapped = pltpu.roll(mine, share, 0)
    first = lax.broadcasted_iota(jnp.int32, mine.shape, 0) < share
    swapped = jnp.where(first, -swapped, swapped)
    nt = (((1,), (1,)), ((), ()))
    out = lax.dot_general(mine, inv[0], nt, precision=lax.Precision.HIGHEST, preferred_element_type=f32)
    out = out + lax.dot_general(swapped, inv[1], nt, precision=lax.Precision.HIGHEST, preferred_element_type=f32)
    solved[...] = out.astype(bf16)

    def along(d):
        return lax.rem(my_site + d, n_site)

    def to_all_sites(src, dst, send, recv):
        copies = []
        for d in range(1, n_site):
            copies.append(pltpu.make_async_remote_copy(
                src_ref=src, dst_ref=dst.at[my_site], send_sem=send.at[d],
                recv_sem=recv.at[d], device_id=(along(d), my_rhs), device_id_type=MESH))
        for copy in copies:
            copy.start()
        dst[my_site] = src[...]
        return copies

    copies = to_all_sites(solved, solved_all, solved_send, solved_recv)
    for copy, relay in zip(defls[1:], relays):
        copy.wait_recv()
        relay.start()

    def coef_sent(d, carry):
        coef_copy(d).wait_send()
        return carry

    lax.fori_loop(1, devices, coef_sent, 0)
    row3 = lax.broadcasted_iota(jnp.int32, (2 * group, 2 * group), 0)
    col3 = lax.broadcasted_iota(jnp.int32, (2 * group, 2 * group), 1)
    slot3 = row3 % group
    want = (slot3 // share) * (2 * share) + (row3 // group) * share + slot3 % share
    sort = jnp.where(col3 == want, 1.0, 0.0).astype(bf16)
    for copy in copies:
        copy.wait()
    low = solved_all[...].astype(f32).reshape(2 * group, vecs).astype(bf16)
    low = jnp.dot(sort, low, preferred_element_type=f32).astype(bf16)
    for copy in packs + defls[:1] + relays:
        copy.wait()
    for copy in defls[1:]:
        copy.wait_send()
    anchor = my_site * sites_here - reach
    halves = (range(reach), range(reach, sites_here))

    def keep(step, i, values):
        for buf in bufs[step]:
            buf[reach + i] = values

    def halo(step, half):
        own_buf, out_buf = bufs[step]
        if half == 0:
            source, target, to = out_buf.at[pl.ds(reach, reach)], out_buf.at[pl.ds(reach + sites_here, reach)], n_site - 1
        else:
            source, target, to = own_buf.at[pl.ds(sites_here, reach)], own_buf.at[pl.ds(0, reach)], 1
        copy = pltpu.make_async_remote_copy(
            src_ref=source, dst_ref=target,
            send_sem=halo_send.at[2 * step + half], recv_sem=halo_recv.at[2 * step + half],
            device_id=(along(to), my_rhs), device_id_type=MESH)
        copy.start()
        return copy

    def operate(step, i):
        buf = bufs[step][i // reach]
        pieces = [buf[reach + i]]
        for m in range(nb.shape[0]):
            pieces.append(buf[(nb[m, i] - anchor) & (2 * sites_here - 1)])
        stacked = jnp.concatenate(pieces, axis=1)
        return jnp.dot(stacked, coup[i], preferred_element_type=f32)

    copies = []
    for half in (0, 1):
        for i in halves[half]:
            z = jnp.dot(low, gathered[i], preferred_element_type=f32)
            start = (z[:group] + lanes_turned(z[group:], False)).astype(bf16)
            keep(0, i, start)
            sol_ref[i] = start.astype(f32)
        copies.append(halo(0, half))
    load_nb.wait()
    load_coup.wait()
    later = [None, None]
    for half in (1, 0):
        copies[1 - half].wait_recv()
        for i in halves[half]:
            r = given[i].astype(f32) - operate(0, i)
            first_res[i] = r
            keep(1, i, r.astype(bf16))
        later[half] = halo(1, half)
    sent = copies + later

    lane = lax.broadcasted_iota(jnp.int32, (8, width), 1)
    bands = group // 8

    def apply(step, half, held, into, tops, low_too):
        for i in halves[half]:
            y = operate(step, i)
            r = held[i]
            into[i] = y
            if low_too:
                keep(2, i, y.astype(bf16))
            tops[0] = tops[0] + y * r
            tops[1] = tops[1] + y * lanes_turned(r, True)
            tops[2] = tops[2] + y * y

    def send_sums(step, tops):
        tile = jnp.zeros((8, width), f32)
        for v in range(3):
            column = jnp.sum(tops[v], axis=1, keepdims=True)
            for b in range(bands):
                tile = jnp.where(lane == 3 * b + v, column[8 * b:8 * b + 8], tile)
        sums[step] = tile
        return to_all_sites(sums.at[step], sums_all.at[step], sums_send.at[step], sums_recv.at[step])

    def alphas(step, waits):
        for copy in waits:
            copy.wait()
        tile = jnp.sum(sums_all[step], axis=0)
        values = []
        for v in range(3):
            values.append(jnp.concatenate([tile[:, 3 * b + v:3 * b + v + 1] for b in range(bands)], axis=0))
        alpha_re = jnp.broadcast_to(values[0] / values[2], (group, width))
        alpha_im = jnp.broadcast_to(values[1] / values[2], (group, width))
        return lambda vectors: alpha_re * vectors + alpha_im * lanes_turned(vectors, False)

    tops = [jnp.zeros((group, width), f32) for _ in range(3)]
    beside = []
    for half in (0, 1):
        later[1 - half].wait_recv()
        apply(1, half, first_res, image, tops, True)
        if half == 0:
            beside.append(halo(2, 0))
    waits = send_sums(0, tops)
    beside.append(halo(2, 1))
    first_scaled = alphas(0, waits)
    for i in range(sites_here):
        r = first_res[i] - first_scaled(image[i])
        res_ref[i] = r
        keep(3, i, r.astype(bf16))
    for half in (1, 0):
        beside[1 - half].wait_recv()
        at = (0, reach + sites_here)[half]
        for i in range(reach):
            r = bufs[1][half][at + i].astype(f32) - first_scaled(bufs[2][half][at + i].astype(f32))
            bufs[3][half][at + i] = r.astype(bf16)
    tops = [jnp.zeros((group, width), f32) for _ in range(3)]
    for half in (1, 0):
        apply(3, half, res_ref, image, tops, False)
    waits = send_sums(1, tops)
    for i in range(sites_here):
        sol_ref[i] = sol_ref[i] + first_scaled(first_res[i])
    for copy in sent + beside:
        copy.wait_send()
    second_scaled = alphas(1, waits)
    for i in range(sites_here):
        r = res_ref[i]
        rows = pl.ds(i, group, stride=sites_here)
        sol_out[rows, :] = sol_ref[i] + second_scaled(r)
        res_out[rows, :] = r - second_scaled(image[i])


def fused(n_site, n_rhs, rhs_vecs, deflation, coarse_inverse, coupling, neighbours, grouping):
    f32, bf16 = jnp.float32, jnp.bfloat16
    slots, sites_local, width = rhs_vecs.shape
    vecs = deflation.shape[0]
    sites_here = coupling.shape[0]
    group = slots // n_rhs
    share = group // n_site
    devices = n_site * n_rhs
    blocks = coupling.reshape(sites_here, -1, width)
    vmem = pl.BlockSpec(memory_space=pltpu.VMEM)
    hbm = pl.BlockSpec(memory_space=pltpu.HBM)
    out = pltpu.VMEM((group * sites_here, width), f32)
    dma = pltpu.SemaphoreType.DMA
    sol, res = pl.pallas_call(
        functools.partial(fused_kernel, n_site, n_rhs),
        out_shape=(out, out),
        in_specs=[hbm, hbm, hbm, hbm, hbm, vmem],
        out_specs=(vmem, vmem),
        scratch_shapes=[
            pltpu.VMEM((sites_here, group, width), f32),
            pltpu.VMEM((sites_here, group, width), f32),
            pltpu.VMEM((slots * sites_local, width), bf16),
            pltpu.VMEM((vecs * sites_local, width), bf16),
            pltpu.VMEM((vecs * sites_local, width), f32),
            pltpu.VMEM(coarse_inverse.shape, f32),
            pltpu.SMEM(neighbours.shape[::-1], jnp.int32),
            pltpu.VMEM(blocks.shape, bf16),
            pltpu.VMEM((sites_here, vecs, width), bf16),
            pltpu.VMEM((sites_local, slots, width), bf16),
            pltpu.VMEM((sites_here, group, width), bf16),
            pltpu.VMEM((devices, 2 * share, vecs), bf16),
            pltpu.VMEM((devices, 2 * share, vecs), bf16),
            pltpu.VMEM((2 * share, vecs), bf16),
            pltpu.VMEM((n_site, 2 * share, vecs), bf16),
            pltpu.VMEM((2 * sites_here, group, width), bf16),
            pltpu.VMEM((2 * sites_here, group, width), bf16),
            pltpu.VMEM((2 * sites_here, group, width), bf16),
            pltpu.VMEM((2 * sites_here, group, width), bf16),
            pltpu.VMEM((2 * sites_here, group, width), bf16),
            pltpu.VMEM((2 * sites_here, group, width), bf16),
            pltpu.VMEM((2 * sites_here, group, width), bf16),
            pltpu.VMEM((2 * sites_here, group, width), bf16),
            pltpu.VMEM((sites_here, group, width), f32),
            pltpu.VMEM((sites_here, group, width), f32),
            pltpu.VMEM((2, 8, width), f32),
            pltpu.VMEM((2, n_site, 8, width), f32),
            dma, dma, dma, dma, dma, dma((devices,)), dma((devices,)), dma((n_rhs,)), dma((n_rhs,)),
            dma((n_rhs,)), dma((n_rhs,)), dma((n_site,)), dma((n_site,)),
            dma((6,)), dma((6,)), dma((2, n_site)), dma((2, n_site)),
        ],
        compiler_params=pltpu.CompilerParams(
            collective_id=0, has_side_effects=True, vmem_limit_bytes=62 * 1024 * 1024),
    )(
        rhs_vecs.reshape(slots * sites_local, width),
        deflation.reshape(vecs * sites_local, width),
        coarse_inverse,
        blocks,
        neighbours.T,
        grouping.reshape(1, slots),
    )
    shape = (group, sites_here, width)
    return sol.reshape(shape), res.reshape(shape)


def fits(n_site, n_rhs, rhs_vecs, coupling):
    slots, sites_local, width = rhs_vecs.shape
    sites_here = coupling.shape[0]
    group = slots // n_rhs
    share = group // n_site
    return (
        share * n_site * n_rhs == slots
        and (2 * share) % 8 == 0
        and group % 16 == 0
        and 3 * (group // 8) <= width
        and slots % 128 == 0
        and width % 128 == 0
        and sites_local * n_rhs == sites_here
        and n_site >= 3
        and n_rhs % 2 == 0
        and n_site % 2 == 0
        and sites_here & (sites_here - 1) == 0
    )


def per_device(n_site, n_rhs, *arrays):
    if fits(n_site, n_rhs, arrays[0], arrays[3]):
        return fused(n_site, n_rhs, *arrays)
    return staged(*arrays)


def solution(mesh):
    return jax.shard_map(
        functools.partial(per_device, mesh.shape["site"], mesh.shape["rhs"]),
        mesh=mesh,
        in_specs=(
            P(None, ("site", "rhs"), None),
            P(None, ("site", "rhs"), None),
            P(),
            P("site", None, None, None),
            P("site", None),
            P(),
        ),
        out_specs=(P("rhs", "site", None), P("rhs", "site", None)),
        check_vma=False,
    )
```

```python
import functools

import jax
import jax.numpy as jnp
from jax import lax
from jax.experimental import pallas as pl
from jax.experimental.pallas import tpu as pltpu
from jax.sharding import PartitionSpec as P

MESH = pl.DeviceIdType.MESH
MR_STEPS = 2


def extended_2(array, sides, width):
    for axis, dim in sides:
        size, length = (lax.axis_size(axis), array.shape[dim])
        up = [(i, (i + 1) % size) for i in range(size)]
        down = [(j, i) for i, j in up]
        last = lax.slice_in_dim(array, length - width, length, axis=dim)
        first = lax.slice_in_dim(array, 0, width, axis=dim)
        before = lax.ppermute(last, axis, up)
        after = lax.ppermute(first, axis, down)
        array = jnp.concatenate([before, array, after], axis=dim)
    return array


def turned(vectors):
    half_width = vectors.shape[-1] // 2
    return jnp.concatenate([-vectors[..., half_width:], vectors[..., :half_width]], axis=-1)


def conj_turned(vectors):
    half_width = vectors.shape[-1] // 2
    return jnp.concatenate([vectors[..., half_width:], -vectors[..., :half_width]], axis=-1)


def scaled(alpha_re, alpha_im, vectors):
    return alpha_re[:, None, None] * vectors + alpha_im[:, None, None] * turned(vectors)


def small_solve(coarse_inverse, coef_re, coef_im):
    highest = lax.Precision.HIGHEST
    real_part = coarse_inverse[0]
    imag_part = coarse_inverse[1]
    solved_re = jnp.dot(
        real_part, coef_re, precision=highest, preferred_element_type=jnp.float32
    ) - jnp.dot(imag_part, coef_im, precision=highest, preferred_element_type=jnp.float32)
    solved_im = jnp.dot(
        real_part, coef_im, precision=highest, preferred_element_type=jnp.float32
    ) + jnp.dot(imag_part, coef_re, precision=highest, preferred_element_type=jnp.float32)
    return (solved_re, solved_im)


def operate(vectors, coupling, neighbours):
    slots = vectors.shape[0]
    sites_here = vectors.shape[1]
    width = vectors.shape[2]
    reach = sites_here // 2
    extended = extended_2(vectors, (("site", 1),), reach)
    anchor = lax.axis_index("site") * sites_here
    total = sites_here * lax.axis_size("site")
    position = (neighbours - anchor + reach) % total
    beside = jnp.take(extended, position.reshape(-1), axis=1).reshape(slots, sites_here, 8, width)
    stacked = jnp.concatenate([vectors[:, :, None, :], beside], axis=2).reshape(
        slots, sites_here, 9 * width
    )
    blocks = coupling.reshape(sites_here, 9 * width, width)
    product = lax.dot_general(
        stacked, blocks, (((2,), (1,)), ((1,), (0,))), preferred_element_type=jnp.float32
    )
    return jnp.transpose(product, (1, 0, 2))


def staged(rhs_vecs, deflation, coarse_inverse, coupling, neighbours, grouping):
    ordered = jnp.take(rhs_vecs, grouping, axis=0)
    coef_re = jnp.einsum("ksc,rsc->kr", deflation, ordered, preferred_element_type=jnp.float32)
    coef_im = jnp.einsum(
        "ksc,rsc->kr", deflation, conj_turned(ordered), preferred_element_type=jnp.float32
    )
    group_re, group_im = (
        lax.psum_scatter(coef_re, "rhs", scatter_dimension=1, tiled=True),
        lax.psum_scatter(coef_im, "rhs", scatter_dimension=1, tiled=True),
    )
    group_re, group_im = lax.psum((group_re, group_im), "site")
    share_re, share_im = small_solve(coarse_inverse, group_re, group_im)
    solved_re, solved_im = (
        lax.all_gather(share_re.astype(jnp.bfloat16), "rhs", axis=1, tiled=True).astype(
            share_re.dtype
        ),
        lax.all_gather(share_im.astype(jnp.bfloat16), "rhs", axis=1, tiled=True).astype(
            share_im.dtype
        ),
    )
    low_re = solved_re.astype(jnp.bfloat16)
    low_im = solved_im.astype(jnp.bfloat16)
    start = jnp.einsum("kr,ksc->rsc", low_re, deflation, preferred_element_type=jnp.float32)
    start = start + jnp.einsum(
        "kr,ksc->rsc", low_im, turned(deflation), preferred_element_type=jnp.float32
    )
    start_low = start.astype(jnp.bfloat16)
    given_low, placed = (
        lax.all_to_all(ordered, "rhs", split_axis=0, concat_axis=1, tiled=True),
        lax.all_to_all(start_low, "rhs", split_axis=0, concat_axis=1, tiled=True),
    )
    given = given_low.astype(jnp.float32)
    solution = placed.astype(jnp.float32)
    residual = given - operate(placed, coupling, neighbours)
    for iteration in range(MR_STEPS):
        image = operate(residual.astype(jnp.bfloat16), coupling, neighbours)
        upper_re = jnp.sum(image * residual, axis=(1, 2))
        upper_im = jnp.sum(image * conj_turned(residual), axis=(1, 2))
        lower = jnp.sum(image * image, axis=(1, 2))
        upper_re, upper_im, lower = lax.psum((upper_re, upper_im, lower), "site")
        alpha_re = upper_re / lower
        alpha_im = upper_im / lower
        solution = solution + scaled(alpha_re, alpha_im, residual)
        residual = residual - scaled(alpha_re, alpha_im, image)
    return (solution, residual)


def lanes_turned(values, conj):
    width = values.shape[-1]
    lane = lax.broadcasted_iota(jnp.int32, values.shape, values.ndim - 1)
    rolled = pltpu.roll(values, width // 2, values.ndim - 1)
    low = lane < width // 2
    if conj:
        return jnp.where(low, rolled, -rolled)
    return jnp.where(low, -rolled, rolled)


def fused_kernel(
    n_site, n_rhs,
    rhs_hbm, defl_hbm, inv_hbm, coup_hbm, nb_hbm, group_ref,
    sol_out, res_out,
    sol_ref, res_ref, rhs_ref, defl_ref, wide, inv, nb, coup, gathered, ordered, given, coef, parts, solved, solved_all, low0, high0, low1, high1, low2, high2, low3, high3, first_res, image, sums, sums_all,
    rhs_sem, defl_sem, inv_sem, nb_sem, coup_sem, coef_send, coef_recv, pack_send, pack_recv, defl_send, defl_recv,
    solved_send, solved_recv, halo_send, halo_recv, sums_send, sums_recv,
):
    devices = n_site * n_rhs
    width = rhs_ref.shape[1]
    slots = group_ref.shape[1]
    sites_local = rhs_ref.shape[0] // slots
    sites_here = coup_hbm.shape[0]
    reach = sites_here // 2
    group = slots // n_rhs
    share = group // n_site
    vecs = inv_hbm.shape[1]
    f32, bf16 = jnp.float32, jnp.bfloat16
    bufs = ((low0, high0), (low1, high1), (low2, high2), (low3, high3))

    my_site = lax.axis_index("site")
    my_rhs = lax.axis_index("rhs")
    me = my_rhs * n_site + my_site

    def peer(d):
        at = lax.rem(me + d, devices)
        return at, (lax.rem(at, n_site), at // n_site)

    load_coup = pltpu.make_async_copy(coup_hbm, coup, coup_sem)
    load_nb = pltpu.make_async_copy(nb_hbm, nb, nb_sem)
    load_inv = pltpu.make_async_copy(inv_hbm, inv, inv_sem)
    load_rhs = pltpu.make_async_copy(rhs_hbm, rhs_ref, rhs_sem)
    load_defl = pltpu.make_async_copy(defl_hbm, defl_ref, defl_sem)
    load_defl.start()
    load_rhs.start()
    load_nb.start()
    load_inv.start()
    load_coup.start()
    barrier = pltpu.get_barrier_semaphore()

    def greet(d, carry):
        _, dev = peer(d)
        pl.semaphore_signal(barrier, inc=1, device_id=dev, device_id_type=MESH)
        return carry

    for d in range(1, devices):
        greet(d, 0)
    own = my_rhs * sites_local
    load_defl.wait()
    wide[...] = defl_ref[...].astype(f32)
    basis = []
    for i in range(sites_local):
        block = wide[pl.ds(i, vecs, stride=sites_local), :].astype(bf16)
        gathered[own + i] = block
        basis.append(block)
    basis = jnp.concatenate(basis, axis=1)

    row = lax.broadcasted_iota(jnp.int32, (slots * sites_local, slots), 0)
    wanted = group_ref[...] * sites_local
    tn = (((0,), (0,)), ((), ()))
    row2 = lax.broadcasted_iota(jnp.int32, (2 * slots, slots), 0)
    col2 = lax.broadcasted_iota(jnp.int32, (2 * slots, slots), 1)
    spread = jnp.where(col2 == (row2 // (2 * share)) * share + row2 % share, 1.0, 0.0).astype(bf16)
    part = (lax.broadcasted_iota(jnp.int32, (2 * slots, width), 0) // share) % 2
    both = []
    load_rhs.wait()
    for i in range(sites_local):
        placed = jnp.where(row == wanted + i, 1.0, 0.0).astype(bf16)
        g = lax.dot_general(placed, rhs_ref[...], tn, preferred_element_type=f32).astype(bf16)
        ordered[i] = g
        two = jnp.dot(spread, g, preferred_element_type=f32)
        both.append(jnp.where(part == 1, lanes_turned(two, True), two).astype(bf16))
    both = jnp.concatenate(both, axis=1)
    total = lax.dot_general(both, basis, (((1,), (1,)), ((), ())), preferred_element_type=f32)
    coef[...] = total.reshape(devices, 2 * share, vecs).astype(bf16)

    pl.semaphore_wait(barrier, devices - 1)

    def coef_copy(d):
        at, dev = peer(d)
        return pltpu.make_async_remote_copy(
            src_ref=coef.at[at], dst_ref=parts.at[me], send_sem=coef_send.at[d],
            recv_sem=coef_recv.at[me], device_id=dev, device_id_type=MESH)

    def coef_start(d, carry):
        coef_copy(d).start()
        return carry

    lax.fori_loop(1, devices, coef_start, 0)

    def to_rhs(source, target, other, sends, recvs, d):
        return pltpu.make_async_remote_copy(
            src_ref=source, dst_ref=target, send_sem=sends.at[d], recv_sem=recvs.at[d],
            device_id=(my_site, other), device_id_type=MESH)

    half = n_rhs // 2
    twin = my_rhs + 1 - 2 * lax.rem(my_rhs, 2)
    mine_at = gathered.at[pl.ds(own, sites_local)]
    packs, defls = [], []
    for d in range(1, n_rhs):
        other = lax.rem(my_rhs + d, n_rhs)
        packs.append(to_rhs(
            ordered.at[:, pl.ds(pl.multiple_of(other * group, group), group), :],
            given.at[pl.ds(own, sites_local)], other, pack_send, pack_recv, d))
    defls.append(to_rhs(mine_at, mine_at, twin, defl_send, defl_recv, 0))
    relays = []
    for d in range(1, half):
        other = lax.rem(my_rhs + 2 * d, n_rhs)
        defls.append(to_rhs(mine_at, mine_at, other, defl_send, defl_recv, d))
        came = lax.rem(my_rhs + n_rhs - 2 * d, n_rhs) * sites_local
        block = gathered.at[pl.ds(came, sites_local)]
        relays.append(to_rhs(block, block, twin, defl_send, defl_recv, half + d))
    for copy in defls[1:] + defls[:1] + packs:
        copy.start()
    given[pl.ds(own, sites_local)] = ordered[:, pl.ds(pl.multiple_of(my_rhs * group, group), group), :]
    parts[me] = coef[me]

    def coef_wait(d, carry):
        at, dev = peer(d)
        pltpu.make_async_remote_copy(
            src_ref=coef.at[at], dst_ref=parts.at[at], send_sem=coef_send.at[d],
            recv_sem=coef_recv.at[at], device_id=dev, device_id_type=MESH).wait_recv()
        return carry

    lax.fori_loop(1, devices, coef_wait, 0)
    mine = jnp.sum(parts[...].astype(f32), axis=0)
    load_inv.wait()
    swapped = pltpu.roll(mine, share, 0)
    first = lax.broadcasted_iota(jnp.int32, mine.shape, 0) < share
    swapped = jnp.where(first, -swapped, swapped)
    nt = (((1,), (1,)), ((), ()))
    out = lax.dot_general(mine, inv[0], nt, precision=lax.Precision.HIGHEST, preferred_element_type=f32)
    out = out + lax.dot_general(swapped, inv[1], nt, precision=lax.Precision.HIGHEST, preferred_element_type=f32)
    solved[...] = out.astype(bf16)

    def along(d):
        return lax.rem(my_site + d, n_site)

    def to_all_sites(src, dst, send, recv):
        copies = []
        for d in range(1, n_site):
            copies.append(pltpu.make_async_remote_copy(
                src_ref=src, dst_ref=dst.at[my_site], send_sem=send.at[d],
                recv_sem=recv.at[d], device_id=(along(d), my_rhs), device_id_type=MESH))
        for copy in copies:
            copy.start()
        dst[my_site] = src[...]
        return copies

    copies = to_all_sites(solved, solved_all, solved_send, solved_recv)
    for copy, relay in zip(defls[1:], relays):
        copy.wait_recv()
        relay.start()

    def coef_sent(d, carry):
        coef_copy(d).wait_send()
        return carry

    lax.fori_loop(1, devices, coef_sent, 0)
    row3 = lax.broadcasted_iota(jnp.int32, (2 * group, 2 * group), 0)
    col3 = lax.broadcasted_iota(jnp.int32, (2 * group, 2 * group), 1)
    slot3 = row3 % group
    want = (slot3 // share) * (2 * share) + (row3 // group) * share + slot3 % share
    sort = jnp.where(col3 == want, 1.0, 0.0).astype(bf16)
    for copy in copies:
        copy.wait()
    low = solved_all[...].astype(f32).reshape(2 * group, vecs).astype(bf16)
    low = jnp.dot(sort, low, preferred_element_type=f32).astype(bf16)
    for copy in defls[:1] + relays:
        copy.wait()
    for copy in defls[1:]:
        copy.wait_send()
    anchor = my_site * sites_here - reach
    halves = (range(reach), range(reach, sites_here))

    def keep(step, i, values):
        for buf in bufs[step]:
            buf[reach + i] = values

    def halo(step, half):
        own_buf, out_buf = bufs[step]
        if half == 0:
            source, target, to = out_buf.at[pl.ds(reach, reach)], out_buf.at[pl.ds(reach + sites_here, reach)], n_site - 1
        else:
            source, target, to = own_buf.at[pl.ds(sites_here, reach)], own_buf.at[pl.ds(0, reach)], 1
        copy = pltpu.make_async_remote_copy(
            src_ref=source, dst_ref=target,
            send_sem=halo_send.at[2 * step + half], recv_sem=halo_recv.at[2 * step + half],
            device_id=(along(to), my_rhs), device_id_type=MESH)
        copy.start()
        return copy

    def operate(step, i):
        buf = bufs[step][i // reach]
        pieces = [buf[reach + i]]
        for m in range(nb.shape[0]):
            pieces.append(buf[(nb[m, i] - anchor) & (2 * sites_here - 1)])
        stacked = jnp.concatenate(pieces, axis=1)
        return jnp.dot(stacked, coup[i], preferred_element_type=f32)

    copies = []
    for half in (0, 1):
        for i in halves[half]:
            z = jnp.dot(low, gathered[i], preferred_element_type=f32)
            start = (z[:group] + lanes_turned(z[group:], False)).astype(bf16)
            keep(0, i, start)
            sol_ref[i] = start.astype(f32)
        copies.append(halo(0, half))
    load_nb.wait()
    load_coup.wait()
    for copy in packs:
        copy.wait()
    later = [None, None]
    for half in (1, 0):
        copies[1 - half].wait_recv()
        for i in halves[half]:
            r = given[i].astype(f32) - operate(0, i)
            first_res[i] = r
            keep(1, i, r.astype(bf16))
        later[half] = halo(1, half)
    sent = copies + later

    lane = lax.broadcasted_iota(jnp.int32, (8, width), 1)
    bands = group // 8

    def apply(step, half, held, into, tops, low_too):
        for i in halves[half]:
            y = operate(step, i)
            r = held[i]
            into[i] = y
            if low_too:
                keep(2, i, y.astype(bf16))
            tops[0] = tops[0] + y * r
            tops[1] = tops[1] + y * lanes_turned(r, True)
            tops[2] = tops[2] + y * y

    def send_sums(step, tops):
        tile = jnp.zeros((8, width), f32)
        for v in range(3):
            column = jnp.sum(tops[v], axis=1, keepdims=True)
            for b in range(bands):
                tile = jnp.where(lane == 3 * b + v, column[8 * b:8 * b + 8], tile)
        sums[step] = tile
        return to_all_sites(sums.at[step], sums_all.at[step], sums_send.at[step], sums_recv.at[step])

    def alphas(step, waits):
        for copy in waits:
            copy.wait()
        tile = jnp.sum(sums_all[step], axis=0)
        values = []
        for v in range(3):
            values.append(jnp.concatenate([tile[:, 3 * b + v:3 * b + v + 1] for b in range(bands)], axis=0))
        alpha_re = jnp.broadcast_to(values[0] / values[2], (group, width))
        alpha_im = jnp.broadcast_to(values[1] / values[2], (group, width))
        return lambda vectors: alpha_re * vectors + alpha_im * lanes_turned(vectors, False)

    tops = [jnp.zeros((group, width), f32) for _ in range(3)]
    beside = []
    for half in (0, 1):
        later[1 - half].wait_recv()
        apply(1, half, first_res, image, tops, True)
        if half == 0:
            beside.append(halo(2, 0))
    waits = send_sums(0, tops)
    beside.append(halo(2, 1))
    first_scaled = alphas(0, waits)
    for i in range(sites_here):
        r = first_res[i] - first_scaled(image[i])
        res_ref[i] = r
        keep(3, i, r.astype(bf16))
    for half in (1, 0):
        beside[1 - half].wait_recv()
        at = (0, reach + sites_here)[half]
        for i in range(reach):
            r = bufs[1][half][at + i].astype(f32) - first_scaled(bufs[2][half][at + i].astype(f32))
            bufs[3][half][at + i] = r.astype(bf16)
    tops = [jnp.zeros((group, width), f32) for _ in range(3)]
    for half in (1, 0):
        apply(3, half, res_ref, image, tops, False)
    waits = send_sums(1, tops)
    for i in range(sites_here):
        sol_ref[i] = sol_ref[i] + first_scaled(first_res[i])
    for copy in sent + beside:
        copy.wait_send()
    second_scaled = alphas(1, waits)
    for i in range(sites_here):
        r = res_ref[i]
        rows = pl.ds(i, group, stride=sites_here)
        sol_out[rows, :] = sol_ref[i] + second_scaled(r)
        res_out[rows, :] = r - second_scaled(image[i])


def fused(n_site, n_rhs, rhs_vecs, deflation, coarse_inverse, coupling, neighbours, grouping):
    f32, bf16 = jnp.float32, jnp.bfloat16
    slots, sites_local, width = rhs_vecs.shape
    vecs = deflation.shape[0]
    sites_here = coupling.shape[0]
    group = slots // n_rhs
    share = group // n_site
    devices = n_site * n_rhs
    blocks = coupling.reshape(sites_here, -1, width)
    vmem = pl.BlockSpec(memory_space=pltpu.VMEM)
    hbm = pl.BlockSpec(memory_space=pltpu.HBM)
    out = pltpu.VMEM((group * sites_here, width), f32)
    dma = pltpu.SemaphoreType.DMA
    sol, res = pl.pallas_call(
        functools.partial(fused_kernel, n_site, n_rhs),
        out_shape=(out, out),
        in_specs=[hbm, hbm, hbm, hbm, hbm, vmem],
        out_specs=(vmem, vmem),
        scratch_shapes=[
            pltpu.VMEM((sites_here, group, width), f32),
            pltpu.VMEM((sites_here, group, width), f32),
            pltpu.VMEM((slots * sites_local, width), bf16),
            pltpu.VMEM((vecs * sites_local, width), bf16),
            pltpu.VMEM((vecs * sites_local, width), f32),
            pltpu.VMEM(coarse_inverse.shape, f32),
            pltpu.SMEM(neighbours.shape[::-1], jnp.int32),
            pltpu.VMEM(blocks.shape, bf16),
            pltpu.VMEM((sites_here, vecs, width), bf16),
            pltpu.VMEM((sites_local, slots, width), bf16),
            pltpu.VMEM((sites_here, group, width), bf16),
            pltpu.VMEM((devices, 2 * share, vecs), bf16),
            pltpu.VMEM((devices, 2 * share, vecs), bf16),
            pltpu.VMEM((2 * share, vecs), bf16),
            pltpu.VMEM((n_site, 2 * share, vecs), bf16),
            pltpu.VMEM((2 * sites_here, group, width), bf16),
            pltpu.VMEM((2 * sites_here, group, width), bf16),
            pltpu.VMEM((2 * sites_here, group, width), bf16),
            pltpu.VMEM((2 * sites_here, group, width), bf16),
            pltpu.VMEM((2 * sites_here, group, width), bf16),
            pltpu.VMEM((2 * sites_here, group, width), bf16),
            pltpu.VMEM((2 * sites_here, group, width), bf16),
            pltpu.VMEM((2 * sites_here, group, width), bf16),
            pltpu.VMEM((sites_here, group, width), f32),
            pltpu.VMEM((sites_here, group, width), f32),
            pltpu.VMEM((2, 8, width), f32),
            pltpu.VMEM((2, n_site, 8, width), f32),
            dma, dma, dma, dma, dma, dma((devices,)), dma((devices,)), dma((n_rhs,)), dma((n_rhs,)),
            dma((n_rhs,)), dma((n_rhs,)), dma((n_site,)), dma((n_site,)),
            dma((6,)), dma((6,)), dma((2, n_site)), dma((2, n_site)),
        ],
        compiler_params=pltpu.CompilerParams(
            collective_id=0, has_side_effects=True, vmem_limit_bytes=62 * 1024 * 1024),
    )(
        rhs_vecs.reshape(slots * sites_local, width),
        deflation.reshape(vecs * sites_local, width),
        coarse_inverse,
        blocks,
        neighbours.T,
        grouping.reshape(1, slots),
    )
    shape = (group, sites_here, width)
    return sol.reshape(shape), res.reshape(shape)


def fits(n_site, n_rhs, rhs_vecs, coupling):
    slots, sites_local, width = rhs_vecs.shape
    sites_here = coupling.shape[0]
    group = slots // n_rhs
    share = group // n_site
    return (
        share * n_site * n_rhs == slots
        and (2 * share) % 8 == 0
        and group % 16 == 0
        and 3 * (group // 8) <= width
        and slots % 128 == 0
        and width % 128 == 0
        and sites_local * n_rhs == sites_here
        and n_site >= 3
        and n_rhs % 2 == 0
        and n_site % 2 == 0
        and sites_here & (sites_here - 1) == 0
    )


def per_device(n_site, n_rhs, *arrays):
    if fits(n_site, n_rhs, arrays[0], arrays[3]):
        return fused(n_site, n_rhs, *arrays)
    return staged(*arrays)


def solution(mesh):
    return jax.shard_map(
        functools.partial(per_device, mesh.shape["site"], mesh.shape["rhs"]),
        mesh=mesh,
        in_specs=(
            P(None, ("site", "rhs"), None),
            P(None, ("site", "rhs"), None),
            P(),
            P("site", None, None, None),
            P("site", None),
            P(),
        ),
        out_specs=(P("rhs", "site", None), P("rhs", "site", None)),
        check_vma=False,
    )
```
